32 devices in a mesh: gx: 4 (over x, core), gy: 8 (over z, y).
Axes of the slice: x: 2, y: 2, z: 4, core: 2. Of those that a mesh axis runs over, the one named last changes fastest.
Arguments:
- primal_pops: float32 [27, 64, 64, 6], P(None, 'gx', 'gy'), may hold values from 0.2 to 1.8
- tangent_pops: float32 [27, 64, 64, 384], P(None, 'gx', 'gy'), may hold values from -6 to 6
- inflow_pops: float32 [9, 64, 6], replicated, may hold values from 0.2 to 1.8
- inflow_sens: float32 [9, 64, 384], replicated, may hold values from -6 to 6
- w_in: float32 [128, 27], replicated, may hold values from -1.25 to 1.25
- b_in: float32 [128], replicated, may hold values from -3 to 3
- w_mid: float32 [128, 128], replicated, may hold values from -0.5 to 0.5
- b_mid: float32 [128], replicated, may hold values from -3 to 3
- w_out: float32 [27, 128], replicated, may hold values from -0.5 to 0.5
- b_out: float32 [27], replicated, may hold values from -2 to 2
- probe_cells: int32 [32, 32, 4], P(('gx', 'gy')), may hold values from 0 to 767
- probe_counts: int32 [32, 32], P(('gx', 'gy')), may hold values from 0 to 4, as said below
Outputs:
- primal_out: float32 [27, 64, 64, 6], P(None, 'gx', 'gy')
- tangent_out: float32 [27, 64, 64, 384], P(None, 'gx', 'gy')
- jac_rows: float32 [32, 32, 4, 256], P(('gx', 'gy'))
The draws below stay inside these ranges and needn't reach their ends.
Inputs may be any that keep to these rules, and one draw needn't show every extreme that they name: `probe_cells`: a local cell of the holder; slots at or beyond probe_counts for that owner are unused. `probe_counts`: in every draw one owner receives exactly 4 probes from every holder.
All inputs are finite; a program needn't handle non-finite values.
Results may differ from the reference program's by a relative error of at most 0.00011.
Values sent between devices are 32-bit elements; how exact they have to be, the bound alone decides.
A program may use at most 128 MiB of HBM per device.

```python
import jax
import jax.numpy as jnp
import numpy as np
from jax import lax

BX = 16
BY = 8
NZ = 6
K = 64
HID = 128
STEPS = 2
CAP = 4
NX = 64
NY = 64
PEERS = 32
CELLS = 768
N_GY = 8


def draw_probe_counts(key, part):
    counts_drawn = jax.random.randint(jax.random.fold_in(key, 11), (PEERS, PEERS), 0, CAP + 1)
    busiest = jax.random.randint(jax.random.fold_in(key, 12), (), 0, PEERS)
    columns = lax.broadcasted_iota(jnp.int32, (PEERS, PEERS), 1)
    return jnp.where(columns == busiest, CAP, counts_drawn).astype(jnp.int32)


def place_ends(drawn, rng, least, top_value):
    index_at = [jax.random.randint(jax.random.fold_in(rng, axis), (), 0, length) for axis, length in enumerate(drawn.shape)]
    main_axis = drawn.shape.index(max(drawn.shape))
    next_to = index_at[:main_axis] + [(index_at[main_axis] + 1) % drawn.shape[main_axis]] + index_at[main_axis + 1:]
    return drawn.at[tuple(index_at)].set(least).at[tuple(next_to)].set(top_value)


def level_of(stream_key, shape, shards, low, largest):
    def one(axis_at, shards_of):
        heights = jax.random.uniform(jax.random.fold_in(jax.random.fold_in(stream_key, 6), axis_at), (shards_of,), jnp.float32, low / len(shards), largest / len(shards))
        return jnp.repeat(jnp.exp(heights), shape[axis_at] // shards_of).reshape((-1,) + (1,) * (len(shape) - axis_at - 1))

    gain = one(*shards[0])
    for cut in shards[1:]:
        gain = gain * one(*cut)
    return gain


def bell_draw(key, shape, spread, limit, shards=(), kind=jnp.bfloat16):
    factor_of = level_of(key, shape, shards, -0.22, 0.18) if shards else 1.0
    drawn = jax.random.normal(key, shape, jnp.float32) * spread * factor_of
    return jnp.minimum(jnp.maximum(drawn, -limit), limit).astype(kind)


def setup_inputs(seed: int = 0) -> dict:
    arg_keys = jax.random.split(jax.random.key(seed), 13)
    return {
        "primal_pops": jnp.clip(0.2 + 1.5999999 * jax.random.uniform(arg_keys[0], (27, NX, NY, NZ), jnp.float32) ** level_of(arg_keys[0], (27, NX, NY, NZ), ((1, 4), (2, 8)), -0.2, 0.2), 0.2, 1.8),
        "tangent_pops": bell_draw(arg_keys[1], (27, NX, NY, NZ * K), 1.0, 6.0, ((1, 4), (2, 8)), jnp.float32),
        "inflow_pops": jnp.clip(jax.random.uniform(arg_keys[2], (9, NY, NZ), jnp.float32, 0.2, 1.8), 0.2, 1.8),
        "inflow_sens": bell_draw(arg_keys[3], (9, NY, NZ * K), 1.0, 6.0, (), jnp.float32),
        "w_in": bell_draw(arg_keys[4], (HID, 27), 27 ** -0.5, 1.25, (), jnp.float32),
        "b_in": bell_draw(arg_keys[5], (HID,), 0.5, 3.0, (), jnp.float32),
        "w_mid": bell_draw(arg_keys[6], (HID, HID), HID ** -0.5, 0.5, (), jnp.float32),
        "b_mid": bell_draw(arg_keys[7], (HID,), 0.5, 3.0, (), jnp.float32),
        "w_out": bell_draw(arg_keys[8], (27, HID), HID ** -0.5, 0.5, (), jnp.float32),
        "b_out": bell_draw(arg_keys[9], (27,), 0.3, 2.0, (), jnp.float32),
        "probe_cells": place_ends(jax.random.randint(arg_keys[10], (PEERS, PEERS, CAP), 0, CELLS), jax.random.fold_in(arg_keys[10], 1), 0, CELLS - 1).astype(jnp.int32),
        "probe_counts": draw_probe_counts(jax.random.fold_in(arg_keys[12], 71), 0),
    }


precise = lax.Precision.HIGHEST


def lattice_table():
    return np.array([[q // 9 - 1, (q // 3) % 3 - 1, q % 3 - 1] for q in range(27)])


def observe_table():
    lattice = lattice_table()
    return np.concatenate([np.ones((1, 27)), lattice.T], axis=0).astype(np.float32)


def stream_region(post_state, k_width):
    lattice = lattice_table()
    rows_x = post_state.shape[1] - 2
    rows_y = post_state.shape[2] - 2
    result = []
    for q in range(27):
        step_x, step_y, step_z = (int(v) for v in lattice[q])
        shifted = post_state[q, 1 - step_x:1 - step_x + rows_x, 1 - step_y:1 - step_y + rows_y]
        mirror = post_state[26 - q, 1:1 + rows_x, 1:1 + rows_y]
        if step_z == 1:
            shifted = jnp.concatenate([mirror[..., :k_width], shifted[..., :-k_width]], axis=-1)
        elif step_z == -1:
            shifted = jnp.concatenate([shifted[..., k_width:], mirror[..., -k_width:]], axis=-1)
        result.append(shifted)
    return jnp.stack(result)


def ghost_pad(post_state, inflow):
    inflow_layer = jnp.concatenate([jnp.zeros_like(post_state[:18, :1]), inflow[:, None]], axis=0)
    padded = jnp.concatenate([inflow_layer, post_state, post_state[:, -1:]], axis=1)
    return jnp.concatenate([padded[:, :, -1:], padded, padded[:, :, :1]], axis=2)


def collide_row(inputs, w_in, b_in, w_mid, b_mid, w_out, b_out):
    cell_state, tangent_row = inputs
    span_y, z_depth = cell_state.shape[1], cell_state.shape[2]
    k_width = tangent_row.shape[2] // z_depth
    first = jnp.einsum('hq,qyz->hyz', w_in, cell_state, precision=precise) + b_in[:, None, None]
    act_one = jnp.tanh(first)
    second = jnp.einsum('hg,gyz->hyz', w_mid, act_one, precision=precise) + b_mid[:, None, None]
    act_two = jnp.tanh(second)
    new_state = cell_state + jnp.einsum('qh,hyz->qyz', w_out, act_two, precision=precise) + b_out[:, None, None]
    slope_one = 1.0 - act_one * act_one
    slope_two = 1.0 - act_two * act_two
    outer_part = w_out[:, :, None, None] * slope_two[None]
    middle_part = jnp.einsum('qhyz,hg->qgyz', outer_part, w_mid, precision=precise) * slope_one[None]
    cell_matrix = jnp.einsum('qgyz,gp->qpyz', middle_part, w_in, precision=precise)
    tangent_four = tangent_row.reshape(27, span_y, z_depth, k_width)
    new_tangent = tangent_four + jnp.einsum('qpyz,pyzk->qyzk', cell_matrix, tangent_four, precision=precise)
    return new_state, new_tangent.reshape(27, span_y, z_depth * k_width)


def reference(primal_pops, tangent_pops, inflow_pops, inflow_sens, w_in, b_in, w_mid, b_mid, w_out, b_out, probe_cells, probe_counts):
    primal, tangent = primal_pops, tangent_pops
    for step_index in range(STEPS):
        def row_update(inputs):
            return collide_row(inputs, w_in, b_in, w_mid, b_mid, w_out, b_out)
        new_primal, new_tangent = lax.map(row_update, (jnp.moveaxis(primal, 1, 0), jnp.moveaxis(tangent, 1, 0)))
        primal = stream_region(ghost_pad(jnp.moveaxis(new_primal, 0, 1), inflow_pops), 1)
        tangent = stream_region(ghost_pad(jnp.moveaxis(new_tangent, 0, 1), inflow_sens), K)
    observe = jnp.asarray(observe_table(), jnp.float32)
    observed = jnp.einsum('oq,qxyw->oxyw', observe, tangent, precision=precise)
    grid = observed.reshape(4, NX, NY, NZ, K)
    holder = jnp.arange(PEERS, dtype=jnp.int32)[:, None, None]
    place_x = (holder // N_GY) * BX + probe_cells // (BY * NZ)
    place_y = (holder % N_GY) * BY + (probe_cells // NZ) % BY
    place_z = probe_cells % NZ
    picked = grid[:, place_x, place_y, place_z, :]
    ordered = jnp.transpose(picked, (2, 1, 3, 0, 4)).reshape(PEERS, PEERS, CAP, 4 * K)
    slot_index = jnp.arange(CAP, dtype=jnp.int32)[None, None, :]
    live_slot = slot_index < jnp.transpose(probe_counts)[:, :, None]
    jac_rows = jnp.where(live_slot[..., None], ordered, jnp.zeros_like(ordered))
    return primal, tangent, jac_rows
```

```python
import functools

import jax
import jax.numpy as jnp
from jax import lax
from jax.experimental import pallas as pl
from jax.experimental.pallas import tpu as pltpu
from jax.sharding import PartitionSpec as P

STEPS = 2
QS = 32
LANES = 128
ROWS_Y = 8
CHUNK = 9
VMEM_LIMIT = 60 * 1024 * 1024
LATTICE = [(q // 9 - 1, q // 3 % 3 - 1, q % 3 - 1) for q in range(27)]


def split(value):
    high = value.astype(jnp.bfloat16)
    low = (value - high.astype(jnp.float32)).astype(jnp.bfloat16)
    return high, low


def dot(a, b):
    return jnp.dot(a, b, preferred_element_type=jnp.float32)


def lane_iota(rows):
    return lax.broadcasted_iota(jnp.int32, (rows, LANES), 1)


def sublane_iota(rows):
    return lax.broadcasted_iota(jnp.int32, (rows, LANES), 0)


def fill(value, rows, columns):
    if value.shape[1] < columns:
        value = jnp.concatenate([value, jnp.zeros((value.shape[0], columns - value.shape[1]), value.dtype)], axis=1)
    if value.shape[0] < rows:
        value = jnp.concatenate([value, jnp.zeros((rows - value.shape[0], columns), value.dtype)], axis=0)
    return value


def three_products(weight):
    high, low = split(weight)
    return jnp.concatenate(
        [jnp.concatenate([high, low], axis=1), jnp.concatenate([high, jnp.zeros_like(low)], axis=1)], axis=0
    )


def times(value, weight):
    high, low = split(value)
    both = dot(jnp.concatenate([high, low], axis=1), weight[...])
    return both[:, :LANES] + both[:, LANES:]


def make_weights(w_in_t, w_mid, w_out, lift, mix, drop, mid, pull):
    turned_in = fill(w_in_t[...], LANES, LANES)
    lift[...] = three_products(turned_in)
    mix[...] = three_products(jnp.transpose(w_mid[...]))
    drop[...] = three_products(jnp.transpose(fill(w_out[...], LANES, LANES)))
    mid[...] = three_products(w_mid[...])
    top = turned_in[:QS]
    high = top.astype(jnp.bfloat16).astype(jnp.float32)
    wide = jnp.transpose(jnp.concatenate([high, top - high, high, high], axis=0))
    lane = lane_iota(LANES)
    only_high = jnp.where((lane >= QS) & (lane < 2 * QS), 0.0, wide)
    pull[...] = jnp.concatenate([wide, only_high], axis=0).astype(jnp.bfloat16)


def primal_collide(cells, post, slope_one, slope_two, biases, lift, mix, drop):
    rows_x, plane = cells.shape[0], cells.shape[1]
    bias_in, bias_mid, bias_out = biases
    block = 4

    def rows(i, carry):
        at = pl.multiple_of(i * block, block)
        cell = cells[pl.ds(at, block)].reshape(block * plane, LANES)
        act_one = jnp.tanh(times(cell, lift) + bias_in)
        act_two = jnp.tanh(times(act_one, mix) + bias_mid)
        after = cell + times(act_two, drop) + bias_out
        slope_one[pl.ds(at, block)] = (1.0 - act_one * act_one).reshape(block, plane, LANES)
        slope_two[pl.ds(at, block)] = (1.0 - act_two * act_two).reshape(block, plane, LANES)
        post[pl.ds(at + 1, block)] = after.reshape(block, plane, LANES)
        return carry

    lax.fori_loop(0, rows_x // block, rows, 0)


def primal_stream(post, sides, mirror, write, z_depth):
    rows_x = post.shape[0] - 2
    lane, at_y = lane_iota(ROWS_Y), sublane_iota(ROWS_Y)
    plus_x, minus_x = (lane >= 18) & (lane < 27), lane < 9
    step_y, step_z = lane // 3 % 3, lane % 3
    turn = jnp.where((lane_iota(LANES) + sublane_iota(LANES) == 26), 1.0, 0.0).astype(jnp.bfloat16)
    turn = jnp.concatenate([turn, turn], axis=0)
    for end, z in ((0, 0), (1, z_depth - 1)):
        wall = post[1 : rows_x + 1, z * ROWS_Y : (z + 1) * ROWS_Y, :].reshape(rows_x * ROWS_Y, LANES)
        high, middle = split(wall)
        rest = (wall - high.astype(jnp.float32) - middle.astype(jnp.float32)).astype(jnp.bfloat16)
        turned = dot(jnp.concatenate([high, middle], axis=1), turn) + dot(rest, turn[:LANES])
        mirror[end] = turned.reshape(rows_x, ROWS_Y, LANES)

    def row(x, carry):
        def from_x(take):
            return jnp.where(plus_x, take(x), jnp.where(minus_x, take(x + 2), take(x + 1)))

        low = from_x(lambda i: sides[0, i])
        high = from_x(lambda i: sides[1, i])
        planes = []
        for z in range(z_depth):
            own = from_x(lambda i: post[i, z * ROWS_Y : (z + 1) * ROWS_Y, :])
            up = jnp.where(at_y == 0, low[z : z + 1], pltpu.roll(own, 1, 0))
            down = jnp.where(at_y == ROWS_Y - 1, high[z : z + 1], pltpu.roll(own, ROWS_Y - 1, 0))
            planes.append(jnp.where(step_y == 2, up, jnp.where(step_y == 0, down, own)))
        for z in range(z_depth):
            below = planes[z - 1] if z else mirror[0, x]
            above = planes[z + 1] if z + 1 < z_depth else mirror[1, x]
            write(x, z, jnp.where(step_z == 2, below, jnp.where(step_z == 0, above, planes[z])))
        return carry

    lax.fori_loop(0, rows_x, row, 0)


def jacobians(jac, slope_one, slope_two, w_out, mid, pull):
    rows_x, plane = slope_one.shape[0], slope_one.shape[1]

    def row(x, carry):
        one, two = slope_one[x], slope_two[x]
        for first in range(0, 27, CHUNK):
            outer = (w_out[first : first + CHUNK, :][:, None, :] * two[None]).reshape(CHUNK * plane, LANES)
            middle = times(outer, mid)
            middle = (middle.reshape(CHUNK, plane, LANES) * one[None]).reshape(CHUNK * plane, LANES)
            high, low = split(middle)
            jac[x, first * plane : (first + CHUNK) * plane, :] = dot(jnp.concatenate([high, low], axis=1), pull[...])
        return carry

    lax.fori_loop(0, rows_x, row, 0, unroll=2)


def move_columns(x, columns, jac, state, post, plane):
    lane = lane_iota(QS)
    left, low_part = lane < LANES // 2, (lane >= 2 * QS) & (lane < 3 * QS)

    def cell_rows(y, z):
        rows = jac[x, pl.ds(z * ROWS_Y + y, QS, stride=plane), :]
        high = rows.astype(jnp.bfloat16).astype(jnp.float32)
        return jnp.where(low_part, rows - high, rows).astype(jnp.bfloat16)

    for y, pair in columns:
        cell = state[x, pair, pl.ds(y, QS, stride=ROWS_Y), :]
        high, low = split(cell)
        none = jnp.zeros_like(high)
        parts = []
        for keep in (lambda v: jnp.where(left, v, none), lambda v: jnp.where(left, none, v)):
            parts += [keep(high)] * 3 + [keep(low)]
        rows = jnp.concatenate([cell_rows(y, 2 * pair), cell_rows(y, 2 * pair + 1)], axis=1)
        post[x, pair, pl.ds(y, QS, stride=ROWS_Y), :] = cell + dot(rows, jnp.concatenate(parts, axis=0))


def stream_rows(before, x_rows, sides, write):
    rows_x, pairs = before.shape[0], before.shape[1]
    rows_y = ROWS_Y
    lane = lane_iota(rows_y)
    left = lane < LANES // 2
    at_y = lax.broadcasted_iota(jnp.int32, (rows_y, LANES), 0)
    def one_row(x, edge):
        for q, (ex, ey, ez) in enumerate(LATTICE):
            parts = []
            for pair in range(pairs):
                if edge == -1 and ex == 1:
                    value = x_rows[0, q - 18, pair]
                elif edge == 1 and ex == -1:
                    value = x_rows[1, q, pair]
                else:
                    value = before[x - ex, pair, q * rows_y : (q + 1) * rows_y, :]
                if ey != 0:
                    j = (ex + 1) * 3 + ez + 1
                    side = sides[0 if ey == 1 else 1, j, pair, pl.ds(x - ex + 1, 1), :]
                    if ey == 1:
                        value = jnp.where(at_y == 0, side, pltpu.roll(value, 1, 0))
                    else:
                        value = jnp.where(at_y == rows_y - 1, side, pltpu.roll(value, rows_y - 1, 0))
                parts.append(value)
            if ez != 0:
                turned = [pltpu.roll(part, LANES // 2, 1) for part in parts]
                mirror = 26 - q
                if ez == 1:
                    wall = before[x, 0, mirror * rows_y : (mirror + 1) * rows_y, :]
                    parts = [jnp.where(left, turned[p - 1] if p else wall, turned[p]) for p in range(pairs)]
                else:
                    wall = before[x, pairs - 1, mirror * rows_y : (mirror + 1) * rows_y, :]
                    parts = [jnp.where(left, turned[p], turned[p + 1] if p + 1 < pairs else wall) for p in range(pairs)]
            write(x, q, parts)

    one_row(0, -1)

    def inner(x, carry):
        one_row(x, 0)
        return carry

    lax.fori_loop(1, rows_x - 1, inner, 0)
    one_row(rows_x - 1, 1)


def kernel(z_depth, probe_cells, probe_counts, cells_in, inflow, w_in_t, b_in, w_mid, b_mid, w_out, b_out,
           tangent, sens, primal_out, jac_out, tangent_out, *scratch):
    (cells, lift, mix, drop, mid, pull, slope_one, slope_two, turning, inflow_rows, cell_post, cell_sides, mirror,
     cell_edge, cell_face, cell_edge_in, cell_face_in, cell_corner_in, jac, state, post, sens_rows, x_rows, sides,
     edge, face, corner, edge_in, face_in, corner_in, observed, jac_rows, jac_in,
     load_sem, sens_sem, store_sem, send_sem, recv_sem, jac_send_sem, jac_recv_sem) = scratch
    rows_x, pairs, plane = state.shape[0], state.shape[1], cells.shape[1]
    column, columns_x = lax.axis_index("gx"), lax.axis_size("gx")
    line, lines = lax.axis_index("gy"), lax.axis_size("gy")
    me, peers = column * lines + line, columns_x * lines
    first, last = column == 0, column == columns_x - 1
    end = rows_x + 1

    def at(dx, dy):
        return (lax.rem(column + dx + columns_x, columns_x), lax.rem(line + dy + lines, lines))

    barrier = pltpu.get_barrier_semaphore()

    def greet(i, carry):
        other = lax.rem(me + i, peers)
        pl.semaphore_signal(barrier, inc=1, device_id=(other // lines, lax.rem(other, lines)),
                            device_id_type=pl.DeviceIdType.MESH)
        return carry

    lax.fori_loop(1, peers, greet, 0)

    boxes = state.reshape(rows_x, pairs, QS, ROWS_Y, LANES)

    def load(x, pair):
        return pltpu.make_async_copy(
            tangent.at[:, x, :, pl.ds(pair * LANES, LANES)], boxes.at[x, pair, pl.ds(0, 27)], load_sem.at[x, pair])

    def store(x, pair):
        return pltpu.make_async_copy(
            boxes.at[x, pair, pl.ds(0, 27)], tangent_out.at[:, x, :, pl.ds(pair * LANES, LANES)], store_sem.at[x, pair])

    def start_load(x, carry):
        for pair in range(pairs):
            load(x, pair).start()
        return carry

    lax.fori_loop(0, rows_x, start_load, 0)
    sens_copies = []
    for i in range(3):
        from_y = pl.multiple_of(lax.rem(line + i - 1 + lines, lines) * ROWS_Y, ROWS_Y)
        copy = pltpu.make_async_copy(sens.at[:, pl.ds(from_y, ROWS_Y), :], sens_rows.at[i], sens_sem.at[i])
        copy.start()
        sens_copies.append(copy)

    counter = [0]

    def send(source, target, dx, dy):
        i = counter[0]
        counter[0] += 1
        copy = pltpu.make_async_remote_copy(
            src_ref=source, dst_ref=target, send_sem=send_sem.at[i], recv_sem=recv_sem.at[i],
            device_id=at(dx, dy), device_id_type=pl.DeviceIdType.MESH,
        )
        copy.start()
        return copy

    make_weights(w_in_t, w_mid, w_out, lift, mix, drop, mid, pull)
    biases = (b_in[...], b_mid[...], fill(b_out[...], 1, LANES))
    cells[...] = jnp.zeros(cells.shape, jnp.float32)
    cells[:, :, 0:27] = cells_in[...]

    def clear(x, carry):
        jac[x, 27 * plane :, :] = jnp.zeros(((QS - 27) * plane, LANES), jnp.float32)
        for pair in range(pairs):
            state[x, pair, 27 * ROWS_Y :, :] = jnp.zeros(((QS - 27) * ROWS_Y, LANES), jnp.float32)
        return carry

    lax.fori_loop(0, rows_x, clear, 0)

    def send_cells(step):
        for x in range(rows_x):
            for way, y in ((0, 0), (1, ROWS_Y - 1)):
                for z in range(z_depth):
                    cell_face[step, way, x, z : z + 1, :] = cell_post[x + 1, z * ROWS_Y + y : z * ROWS_Y + y + 1, :]
                cell_face[step, way, x, z_depth:, :] = jnp.zeros((8 - z_depth, LANES), jnp.float32)
        cell_edge[step, 0] = cell_post[1]
        cell_edge[step, 1] = cell_post[rows_x]
        return [
            send(cell_edge.at[step, 1], cell_edge_in.at[step, 0], 1, 0),
            send(cell_edge.at[step, 0], cell_edge_in.at[step, 1], -1, 0),
            send(cell_face.at[step, 1], cell_face_in.at[step, 0], 0, 1),
            send(cell_face.at[step, 0], cell_face_in.at[step, 1], 0, -1),
            send(cell_face.at[step, 1, rows_x - 1], cell_corner_in.at[step, 0], 1, 1),
            send(cell_face.at[step, 1, 0], cell_corner_in.at[step, 1], -1, 1),
            send(cell_face.at[step, 0, rows_x - 1], cell_corner_in.at[step, 2], 1, -1),
            send(cell_face.at[step, 0, 0], cell_corner_in.at[step, 3], -1, -1),
        ]

    def finish_cells(step, copies):
        for copy in copies:
            copy.wait()
        start = pl.multiple_of(line * ROWS_Y, ROWS_Y)
        around = (lax.rem(start + lines * ROWS_Y - 1, lines * ROWS_Y), lax.rem(start + ROWS_Y, lines * ROWS_Y))
        for z in range(z_depth):
            rows = slice(z * ROWS_Y, (z + 1) * ROWS_Y)
            cell_post[0, rows, :] = jnp.where(
                first, inflow_rows[z, pl.ds(start, ROWS_Y), :], cell_edge_in[step, 0, rows, :])
            for way in range(2):
                cell_sides[way, 0, z : z + 1, :] = jnp.where(
                    first, inflow_rows[z, pl.ds(around[way], 1), :], cell_corner_in[step, 2 * way, z : z + 1, :])
        cell_post[end] = jnp.where(last, cell_post[rows_x], cell_edge_in[step, 1])
        for way in range(2):
            cell_sides[way, 1:end] = cell_face_in[step, way]
            cell_sides[way, end] = jnp.where(
                last, cell_face_in[step, way, rows_x - 1], cell_corner_in[step, 2 * way + 1])

    def send_columns(step):
        stride = pairs * QS * ROWS_Y
        flat = post.reshape(rows_x * stride, LANES)
        for pair in range(pairs):
            for ex in range(3):
                for ez in range(3):
                    q = ex * 9 + 6 + ez
                    face[step, 1, ex * 3 + ez, pair] = flat[
                        pl.ds((pair * QS + q + 1) * ROWS_Y - 1, rows_x, stride=stride), :]
                    q = ex * 9 + ez
                    face[step, 0, ex * 3 + ez, pair] = flat[pl.ds((pair * QS + q) * ROWS_Y, rows_x, stride=stride), :]
            for j in range(9):
                edge[step, 0, j, pair] = post[0, pair, j * ROWS_Y : (j + 1) * ROWS_Y, :]
                edge[step, 1, j, pair] = post[rows_x - 1, pair, (18 + j) * ROWS_Y : (19 + j) * ROWS_Y, :]
            for i in range(3):
                r = i * pairs + pair
                corner[step, 0, r : r + 1, :] = face[step, 1, 6 + i, pair, rows_x - 1 :, :]
                corner[step, 1, r : r + 1, :] = face[step, 1, i, pair, 0:1, :]
                corner[step, 2, r : r + 1, :] = face[step, 0, 6 + i, pair, rows_x - 1 :, :]
                corner[step, 3, r : r + 1, :] = face[step, 0, i, pair, 0:1, :]
        for c in range(4):
            corner[step, c, 3 * pairs :, :] = jnp.zeros((corner.shape[2] - 3 * pairs, LANES), jnp.float32)
        return [
            send(face.at[step, 1], face_in.at[step, 0], 0, 1),
            send(face.at[step, 0], face_in.at[step, 1], 0, -1),
            send(edge.at[step, 1], edge_in.at[step, 0], 1, 0),
            send(edge.at[step, 0], edge_in.at[step, 1], -1, 0),
            send(corner.at[step, 0], corner_in.at[step, 0], 1, 1),
            send(corner.at[step, 1], corner_in.at[step, 1], -1, 1),
            send(corner.at[step, 2], corner_in.at[step, 2], 1, -1),
            send(corner.at[step, 3], corner_in.at[step, 3], -1, -1),
        ]

    def finish_columns(step, copies):
        for copy in copies:
            copy.wait()
        for pair in range(pairs):
            lanes = slice(pair * LANES, (pair + 1) * LANES)
            for j in range(9):
                own = post[rows_x - 1, pair, j * ROWS_Y : (j + 1) * ROWS_Y, :]
                x_rows[0, j, pair] = jnp.where(first, sens_rows[1, j, :, lanes], edge_in[step, 0, j, pair])
                x_rows[1, j, pair] = jnp.where(last, own, edge_in[step, 1, j, pair])
                for way in range(2):
                    sides[way, j, pair, 1:end] = face_in[step, way, j, pair]
            for way, take in ((0, 6), (1, 0)):
                y = ROWS_Y - 1 if way == 0 else 0
                for i in range(3):
                    r, k = i * pairs + pair, take + i
                    sides[way, 6 + i, pair, 0:1] = jnp.where(
                        first, sens_rows[2 * way, k, y : y + 1, lanes], corner_in[step, 2 * way, r : r + 1, :])
                    sides[way, i, pair, end : end + 1] = jnp.where(
                        last, face_in[step, way, i, pair, rows_x - 1 :, :], corner_in[step, 2 * way + 1, r : r + 1, :])

    inner = [(y, pair) for y in range(1, ROWS_Y - 1) for pair in range(pairs)]
    outer = [(y, pair) for y in (0, ROWS_Y - 1) for pair in range(pairs)]

    def outer_row(x, carry):
        move_columns(x, outer, jac, state, post, plane)
        return carry

    def first_outer_row(x, carry):
        for pair in range(pairs):
            load(x, pair).wait()
        return outer_row(x, carry)

    def inner_row(x, carry):
        move_columns(x, inner, jac, state, post, plane)
        return carry

    def end_row(i, carry):
        return inner_row(i * (rows_x - 1), carry)

    def keep_cells(x, z, value):
        cells[x, z * ROWS_Y : (z + 1) * ROWS_Y, :] = value

    def write_cells(x, z, value):
        primal_out[x, z * ROWS_Y : (z + 1) * ROWS_Y, :] = value[:, :27]

    def keep_columns(x, q, parts):
        for pair in range(pairs):
            state[x, pair, q * ROWS_Y : (q + 1) * ROWS_Y, :] = parts[pair]

    primal_collide(cells, cell_post, slope_one, slope_two, biases, lift, mix, drop)
    pl.semaphore_wait(barrier, peers - 1)
    cell_copies = send_cells(0)
    turning[...] = jnp.zeros(turning.shape, jnp.float32)
    size_y = inflow.shape[2]
    for z in range(z_depth):
        for from_y in range(0, size_y, LANES):
            many = min(LANES, size_y - from_y)
            turning[18:27, 0:many] = inflow[:, z, from_y : from_y + many]
            inflow_rows[z, from_y : from_y + LANES, :] = jnp.transpose(turning[...])
    for copy in sens_copies:
        copy.wait()

    for step in range(STEPS):
        jacobians(jac, slope_one, slope_two, w_out, mid, pull)
        if step:
            finish_columns(step - 1, column_copies)
            stream_rows(post, x_rows, sides, keep_columns)
        lax.fori_loop(0, rows_x, outer_row if step else first_outer_row, 0, unroll=2)
        lax.fori_loop(0, 2, end_row, 0)
        column_copies = send_columns(step)
        lax.fori_loop(1, rows_x - 1, inner_row, 0)
        finish_cells(step, cell_copies)
        if step + 1 < STEPS:
            primal_stream(cell_post, cell_sides, mirror, keep_cells, z_depth)
            primal_collide(cells, cell_post, slope_one, slope_two, biases, lift, mix, drop)
            cell_copies = send_cells(step + 1)
        else:
            primal_stream(cell_post, cell_sides, mirror, write_cells, z_depth)

    sums = {}

    def write(x, q, parts):
        keep_columns(x, q, parts)
        for pair in range(pairs):
            if q == 0:
                sums[pair] = [None] * 4
            held = sums[pair]
            for m, factor in enumerate((1,) + LATTICE[q]):
                if factor == 0:
                    continue
                if held[m] is None:
                    held[m] = parts[pair] if factor == 1 else -parts[pair]
                else:
                    held[m] = held[m] + parts[pair] if factor == 1 else held[m] - parts[pair]
            if q == 26:
                store(x, pair).start()
                for m in range(4):
                    observed[m, pair, pl.ds(pl.multiple_of(x * ROWS_Y, ROWS_Y), ROWS_Y), :] = held[m]

    finish_columns(STEPS - 1, column_copies)
    stream_rows(post, x_rows, sides, write)

    slots = probe_cells.shape[0]
    left = lane_iota(1) < LANES // 2

    def probe(peer, carry):
        for slot in range(slots):
            cell = jnp.clip(probe_cells[slot, peer], 0, observed.shape[2] * z_depth - 1)
            place, z = cell // z_depth, cell % z_depth
            pair, odd = z // 2, z % 2
            live = slot < probe_counts[0, peer]
            rows = [observed[m, pair, pl.ds(place, 1), :] for m in range(4)]
            turned = [pltpu.roll(r, LANES // 2, 1) for r in rows]
            for m in (0, 2):
                low = jnp.where(odd == 1, turned[m], rows[m])
                high = jnp.where(odd == 1, rows[m + 1], turned[m + 1])
                value = jnp.where(left, low, high)
                jac_rows[peer, slot : slot + 1, m * 64 : m * 64 + LANES] = jnp.where(live, value, 0.0)
        return carry

    lax.fori_loop(0, peers, probe, 0, unroll=2)

    def share(other):
        return pltpu.make_async_remote_copy(
            src_ref=jac_rows.at[other], dst_ref=jac_in.at[me], send_sem=jac_send_sem.at[other],
            recv_sem=jac_recv_sem.at[me], device_id=(other // lines, lax.rem(other, lines)),
            device_id_type=pl.DeviceIdType.MESH,
        )

    def take(other):
        return pltpu.make_async_remote_copy(
            src_ref=jac_rows.at[other], dst_ref=jac_in.at[other], send_sem=jac_send_sem.at[other],
            recv_sem=jac_recv_sem.at[other], device_id=(other // lines, lax.rem(other, lines)),
            device_id_type=pl.DeviceIdType.MESH,
        )

    def start_share(i, carry):
        share(lax.rem(me + i, peers)).start()
        return carry

    def end_share(i, carry):
        take(lax.rem(me + i, peers)).wait()
        return carry

    lax.fori_loop(1, peers, start_share, 0)
    jac_in[pl.ds(me, 1)] = jac_rows[pl.ds(me, 1)]
    lax.fori_loop(1, peers, end_share, 0)
    jac_out[...] = jac_in[...]

    def end_store(x, carry):
        for pair in range(pairs):
            store(x, pair).wait()
        return carry

    lax.fori_loop(0, rows_x, end_store, 0)


def shape(*dims):
    return jax.ShapeDtypeStruct(dims, jnp.float32)


def on_device(primal_pops, tangent_pops, inflow_pops, inflow_sens, w_in, b_in, w_mid, b_mid, w_out, b_out,
              probe_cells, probe_counts):
    rows_x, rows_y, z_depth = primal_pops.shape[1:]
    width = tangent_pops.shape[3]
    pairs = width // LANES
    plane = z_depth * rows_y
    size_y = inflow_pops.shape[1]
    padded_y = -(-size_y // LANES) * LANES
    peers, slots = probe_cells.shape[1:]
    columns = 4 * width // z_depth
    corner_rows = -(-3 * pairs // 8) * 8

    cells = jnp.transpose(primal_pops, (1, 3, 2, 0)).reshape(rows_x, plane, 27)
    inflow = jnp.transpose(inflow_pops, (0, 2, 1))
    where_probes = jnp.transpose(probe_cells[0], (1, 0))

    def room(*dims, kind=jnp.float32):
        return pltpu.VMEM(dims, kind)

    def weight(n):
        return room(2 * LANES, n, kind=jnp.bfloat16)

    dma = pltpu.SemaphoreType.DMA
    scratch = [
        room(rows_x, plane, LANES),
        weight(2 * LANES), weight(2 * LANES), weight(2 * LANES), weight(2 * LANES), weight(LANES),
        room(rows_x, plane, LANES),
        room(rows_x, plane, LANES),
        room(LANES, LANES),
        room(z_depth, padded_y, LANES),
        room(rows_x + 2, plane, LANES),
        room(2, rows_x + 2, 8, LANES),
        room(2, rows_x, rows_y, LANES),
        room(STEPS, 2, plane, LANES),
        room(STEPS, 2, rows_x, 8, LANES),
        room(STEPS, 2, plane, LANES),
        room(STEPS, 2, rows_x, 8, LANES),
        room(STEPS, 4, 8, LANES),
        room(rows_x, QS * plane, LANES),
        room(rows_x, pairs, QS * rows_y, LANES),
        room(rows_x, pairs, QS * rows_y, LANES),
        room(3, 9, rows_y, width),
        room(2, 9, pairs, rows_y, LANES),
        room(2, 9, pairs, rows_x + 8, LANES),
        room(STEPS, 2, 9, pairs, rows_y, LANES),
        room(STEPS, 2, 9, pairs, rows_x, LANES),
        room(STEPS, 4, corner_rows, LANES),
        room(STEPS, 2, 9, pairs, rows_y, LANES),
        room(STEPS, 2, 9, pairs, rows_x, LANES),
        room(STEPS, 4, corner_rows, LANES),
        room(4, pairs, rows_x * rows_y, LANES),
        room(peers, slots, columns),
        room(peers, slots, columns),
        dma((rows_x, pairs)),
        dma((3,)),
        dma((rows_x, pairs)),
        dma((16 * STEPS,)),
        dma((16 * STEPS,)),
        dma((peers,)),
        dma((peers,)),
    ]
    smem = pl.BlockSpec(memory_space=pltpu.SMEM)
    vmem = pl.BlockSpec(memory_space=pltpu.VMEM)
    left_out = pl.BlockSpec(memory_space=pl.ANY)
    primal, jac, tangent = pl.pallas_call(
        functools.partial(kernel, z_depth),
        out_shape=(shape(rows_x, plane, 27), shape(peers, slots, columns), shape(*tangent_pops.shape)),
        in_specs=[smem, smem] + [vmem] * 8 + [left_out] * 2,
        out_specs=(vmem, vmem, left_out),
        scratch_shapes=scratch,
        compiler_params=pltpu.CompilerParams(vmem_limit_bytes=VMEM_LIMIT, collective_id=1, has_side_effects=True),
        name="slab",
    )(where_probes, probe_counts, cells, inflow, w_in.T, b_in[None], w_mid, b_mid[None], w_out, b_out[None],
      tangent_pops, inflow_sens)
    primal = jnp.transpose(primal.reshape(rows_x, z_depth, rows_y, 27), (3, 0, 2, 1))
    return primal, tangent, jac[None]


def solution(mesh):
    both = P(("gx", "gy"))
    split_xy = P(None, "gx", "gy", None)
    return jax.shard_map(
        on_device,
        mesh=mesh,
        in_specs=(split_xy, split_xy) + (P(),) * 8 + (both, both),
        out_specs=(split_xy, split_xy, both),
        check_vma=False,
    )
```

```python
import functools

import jax
import jax.numpy as jnp
from jax import lax
from jax.experimental import pallas as pl
from jax.experimental.pallas import tpu as pltpu
from jax.sharding import PartitionSpec as P

STEPS = 2
QS = 32
LANES = 128
ROWS_Y = 8
CHUNK = 9
VMEM_LIMIT = 54 * 1024 * 1024
LATTICE = [(q // 9 - 1, q // 3 % 3 - 1, q % 3 - 1) for q in range(27)]


def split(value):
    high = value.astype(jnp.bfloat16)
    low = (value - high.astype(jnp.float32)).astype(jnp.bfloat16)
    return high, low


def dot(a, b):
    return jnp.dot(a, b, preferred_element_type=jnp.float32)


def lane_iota(rows):
    return lax.broadcasted_iota(jnp.int32, (rows, LANES), 1)


def sublane_iota(rows):
    return lax.broadcasted_iota(jnp.int32, (rows, LANES), 0)


def fill(value, rows, columns):
    if value.shape[1] < columns:
        value = jnp.concatenate([value, jnp.zeros((value.shape[0], columns - value.shape[1]), value.dtype)], axis=1)
    if value.shape[0] < rows:
        value = jnp.concatenate([value, jnp.zeros((rows - value.shape[0], columns), value.dtype)], axis=0)
    return value


def three_products(weight):
    high, low = split(weight)
    return jnp.concatenate(
        [jnp.concatenate([high, low], axis=1), jnp.concatenate([high, jnp.zeros_like(low)], axis=1)], axis=0
    )


def times(value, weight):
    high, low = split(value)
    both = dot(jnp.concatenate([high, low], axis=1), weight[...])
    return both[:, :LANES] + both[:, LANES:]


def make_weights(w_in_t, w_mid, w_out, lift, mix, drop, mid, pull):
    turned_in = fill(w_in_t[...], LANES, LANES)
    lift[...] = three_products(turned_in)
    mix[...] = three_products(jnp.transpose(w_mid[...]))
    drop[...] = three_products(jnp.transpose(fill(w_out[...], LANES, LANES)))
    mid[...] = three_products(w_mid[...])
    top = turned_in[:QS]
    high = top.astype(jnp.bfloat16).astype(jnp.float32)
    wide = jnp.transpose(jnp.concatenate([high, top - high, high, high], axis=0))
    lane = lane_iota(LANES)
    only_high = jnp.where((lane >= QS) & (lane < 2 * QS), 0.0, wide)
    pull[...] = jnp.concatenate([wide, only_high], axis=0).astype(jnp.bfloat16)


def primal_collide(cells, post, slope_one, slope_two, biases, lift, mix, drop):
    rows_x, plane = cells.shape[0], cells.shape[1]
    bias_in, bias_mid, bias_out = biases
    block = 4

    def rows(i, carry):
        at = pl.multiple_of(i * block, block)
        cell = cells[pl.ds(at, block)].reshape(block * plane, LANES)
        act_one = jnp.tanh(times(cell, lift) + bias_in)
        act_two = jnp.tanh(times(act_one, mix) + bias_mid)
        after = cell + times(act_two, drop) + bias_out
        slope_one[pl.ds(at, block)] = (1.0 - act_one * act_one).reshape(block, plane, LANES)
        slope_two[pl.ds(at, block)] = (1.0 - act_two * act_two).reshape(block, plane, LANES)
        post[pl.ds(at + 1, block)] = after.reshape(block, plane, LANES)
        return carry

    lax.fori_loop(0, rows_x // block, rows, 0)


def primal_stream(post, sides, mirror, write, z_depth):
    rows_x = post.shape[0] - 2
    lane, at_y = lane_iota(ROWS_Y), sublane_iota(ROWS_Y)
    plus_x, minus_x = (lane >= 18) & (lane < 27), lane < 9
    step_y, step_z = lane // 3 % 3, lane % 3
    turn = jnp.where((lane_iota(LANES) + sublane_iota(LANES) == 26), 1.0, 0.0).astype(jnp.bfloat16)
    turn = jnp.concatenate([turn, turn], axis=0)
    for end, z in ((0, 0), (1, z_depth - 1)):
        wall = post[1 : rows_x + 1, z * ROWS_Y : (z + 1) * ROWS_Y, :].reshape(rows_x * ROWS_Y, LANES)
        high, middle = split(wall)
        rest = (wall - high.astype(jnp.float32) - middle.astype(jnp.float32)).astype(jnp.bfloat16)
        turned = dot(jnp.concatenate([high, middle], axis=1), turn) + dot(rest, turn[:LANES])
        mirror[end] = turned.reshape(rows_x, ROWS_Y, LANES)

    def row(x, carry):
        def from_x(take):
            return jnp.where(plus_x, take(x), jnp.where(minus_x, take(x + 2), take(x + 1)))

        low = from_x(lambda i: sides[0, i])
        high = from_x(lambda i: sides[1, i])
        planes = []
        for z in range(z_depth):
            own = from_x(lambda i: post[i, z * ROWS_Y : (z + 1) * ROWS_Y, :])
            up = jnp.where(at_y == 0, low[z : z + 1], pltpu.roll(own, 1, 0))
            down = jnp.where(at_y == ROWS_Y - 1, high[z : z + 1], pltpu.roll(own, ROWS_Y - 1, 0))
            planes.append(jnp.where(step_y == 2, up, jnp.where(step_y == 0, down, own)))
        for z in range(z_depth):
            below = planes[z - 1] if z else mirror[0, x]
            above = planes[z + 1] if z + 1 < z_depth else mirror[1, x]
            write(x, z, jnp.where(step_z == 2, below, jnp.where(step_z == 0, above, planes[z])))
        return carry

    lax.fori_loop(0, rows_x, row, 0)


def jacobians(from_x, to_x, jac, slope_one, slope_two, w_out, mid, pull):
    plane, z_depth = slope_one.shape[1], jac.shape[1]

    def row(x, carry):
        one, two = slope_one[x], slope_two[x]
        for first in range(0, 27, CHUNK):
            outer = (w_out[first : first + CHUNK, :][:, None, :] * two[None]).reshape(CHUNK * plane, LANES)
            middle = times(outer, mid)
            middle = (middle.reshape(CHUNK, plane, LANES) * one[None]).reshape(CHUNK * plane, LANES)
            high, low = split(middle)
            ready = dot(jnp.concatenate([high, low], axis=1), pull[...])
            for i in range(CHUNK):
                for z in range(z_depth):
                    at = i * plane + z * ROWS_Y
                    jac[x, z, (first + i) * ROWS_Y : (first + i + 1) * ROWS_Y, :] = ready[at : at + ROWS_Y]
        return carry

    lax.fori_loop(from_x, to_x, row, 0, unroll=2)


def move_columns(x, columns, jac, state, post):
    lane = lane_iota(QS)
    left, low_part = lane < LANES // 2, (lane >= 2 * QS) & (lane < 3 * QS)

    def cell_rows(y, z):
        rows = jac[x, z, pl.ds(y, QS, stride=ROWS_Y), :]
        high = rows.astype(jnp.bfloat16).astype(jnp.float32)
        return jnp.where(low_part, rows - high, rows).astype(jnp.bfloat16)

    for y, pair in columns:
        cell = state[x, pair, pl.ds(y, QS, stride=ROWS_Y), :]
        high, low = split(cell)
        none = jnp.zeros_like(high)
        parts = []
        for keep in (lambda v: jnp.where(left, v, none), lambda v: jnp.where(left, none, v)):
            parts += [keep(high)] * 3 + [keep(low)]
        rows = jnp.concatenate([cell_rows(y, 2 * pair), cell_rows(y, 2 * pair + 1)], axis=1)
        post[x, pair, pl.ds(y, QS, stride=ROWS_Y), :] = cell + dot(rows, jnp.concatenate(parts, axis=0))


def stream_rows(before, x_rows, sides, write):
    rows_x, pairs = before.shape[0], before.shape[1]
    rows_y = ROWS_Y
    lane = lane_iota(rows_y)
    left = lane < LANES // 2
    at_y = lax.broadcasted_iota(jnp.int32, (rows_y, LANES), 0)
    def one_row(x, edge):
        for q, (ex, ey, ez) in enumerate(LATTICE):
            parts = []
            for pair in range(pairs):
                if edge == -1 and ex == 1:
                    value = x_rows[0, q - 18, pair]
                elif edge == 1 and ex == -1:
                    value = x_rows[1, q, pair]
                else:
                    value = before[x - ex, pair, q * rows_y : (q + 1) * rows_y, :]
                if ey != 0:
                    j = (ex + 1) * 3 + ez + 1
                    side = sides[0 if ey == 1 else 1, j, pair, pl.ds(x - ex + 1, 1), :]
                    if ey == 1:
                        value = jnp.where(at_y == 0, side, pltpu.roll(value, 1, 0))
                    else:
                        value = jnp.where(at_y == rows_y - 1, side, pltpu.roll(value, rows_y - 1, 0))
                parts.append(value)
            if ez != 0:
                turned = [pltpu.roll(part, LANES // 2, 1) for part in parts]
                mirror = 26 - q
                if ez == 1:
                    wall = before[x, 0, mirror * rows_y : (mirror + 1) * rows_y, :]
                    parts = [jnp.where(left, turned[p - 1] if p else wall, turned[p]) for p in range(pairs)]
                else:
                    wall = before[x, pairs - 1, mirror * rows_y : (mirror + 1) * rows_y, :]
                    parts = [jnp.where(left, turned[p], turned[p + 1] if p + 1 < pairs else wall) for p in range(pairs)]
            write(x, q, parts)

    one_row(0, -1)

    def inner(x, carry):
        one_row(x, 0)
        return carry

    lax.fori_loop(1, rows_x - 1, inner, 0)
    one_row(rows_x - 1, 1)


def kernel(z_depth, probe_cells, probe_counts, cells_in, inflow, w_in_t, b_in, w_mid, b_mid, w_out, b_out,
           tangent, sens, primal_out, jac_out, state, *scratch):
    (cells, lift, mix, drop, mid, pull, slope_one, slope_two, turning, inflow_rows, cell_post, cell_sides, mirror,
     cell_edge, cell_face, cell_edge_in, cell_face_in, cell_corner_in, jac, post, sens_rows, x_rows, sides,
     edge, face, corner, edge_in, face_in, corner_in, observed, jac_rows, jac_in,
     load_sem, sens_sem, send_sem, recv_sem, jac_send_sem, jac_recv_sem) = scratch
    rows_x, pairs, plane = state.shape[0], state.shape[1], cells.shape[1]
    column, columns_x = lax.axis_index("gx"), lax.axis_size("gx")
    line, lines = lax.axis_index("gy"), lax.axis_size("gy")
    me, peers = column * lines + line, columns_x * lines
    first, last = column == 0, column == columns_x - 1
    end, half = rows_x + 1, rows_x // 2

    def at(dx, dy):
        return (lax.rem(column + dx + columns_x, columns_x), lax.rem(line + dy + lines, lines))

    barrier = pltpu.get_barrier_semaphore()

    def greet(i, carry):
        other = lax.rem(me + i, peers)
        pl.semaphore_signal(barrier, inc=1, device_id=(other // lines, lax.rem(other, lines)),
                            device_id_type=pl.DeviceIdType.MESH)
        return carry

    lax.fori_loop(1, peers, greet, 0)

    boxes = state.reshape(rows_x, pairs, QS, ROWS_Y, LANES)

    def load(x, pair):
        return pltpu.make_async_copy(
            tangent.at[:, x, :, pl.ds(pair * LANES, LANES)], boxes.at[x, pair, pl.ds(0, 27)], load_sem.at[x, pair])

    def start_load(x, carry):
        for pair in range(pairs):
            load(x, pair).start()
        return carry

    lax.fori_loop(0, rows_x, start_load, 0)
    sens_copies = []
    for i in range(3):
        from_y = pl.multiple_of(lax.rem(line + i - 1 + lines, lines) * ROWS_Y, ROWS_Y)
        copy = pltpu.make_async_copy(sens.at[:, pl.ds(from_y, ROWS_Y), :], sens_rows.at[i], sens_sem.at[i])
        copy.start()
        sens_copies.append(copy)

    counter = [0]

    def send(source, target, dx, dy):
        i = counter[0]
        counter[0] += 1
        copy = pltpu.make_async_remote_copy(
            src_ref=source, dst_ref=target, send_sem=send_sem.at[i], recv_sem=recv_sem.at[i],
            device_id=at(dx, dy), device_id_type=pl.DeviceIdType.MESH,
        )
        copy.start()
        return copy

    make_weights(w_in_t, w_mid, w_out, lift, mix, drop, mid, pull)
    biases = (b_in[...], b_mid[...], fill(b_out[...], 1, LANES))
    cells[...] = jnp.zeros(cells.shape, jnp.float32)
    cells[:, :, 0:27] = cells_in[...]

    def clear(x, carry):
        for z in range(z_depth):
            jac[x, z, 27 * ROWS_Y :, :] = jnp.zeros(((QS - 27) * ROWS_Y, LANES), jnp.float32)
        for pair in range(pairs):
            state[x, pair, 27 * ROWS_Y :, :] = jnp.zeros(((QS - 27) * ROWS_Y, LANES), jnp.float32)
        return carry

    lax.fori_loop(0, rows_x, clear, 0)

    def send_cells(step):
        for x in range(rows_x):
            for way, y in ((0, 0), (1, ROWS_Y - 1)):
                for z in range(z_depth):
                    cell_face[step, way, x, z : z + 1, :] = cell_post[x + 1, z * ROWS_Y + y : z * ROWS_Y + y + 1, :]
                cell_face[step, way, x, z_depth:, :] = jnp.zeros((8 - z_depth, LANES), jnp.float32)
        cell_edge[step, 0] = cell_post[1]
        cell_edge[step, 1] = cell_post[rows_x]
        return [
            send(cell_edge.at[step, 1], cell_edge_in.at[step, 0], 1, 0),
            send(cell_edge.at[step, 0], cell_edge_in.at[step, 1], -1, 0),
            send(cell_face.at[step, 1], cell_face_in.at[step, 0], 0, 1),
            send(cell_face.at[step, 0], cell_face_in.at[step, 1], 0, -1),
            send(cell_face.at[step, 1, rows_x - 1], cell_corner_in.at[step, 0], 1, 1),
            send(cell_face.at[step, 1, 0], cell_corner_in.at[step, 1], -1, 1),
            send(cell_face.at[step, 0, rows_x - 1], cell_corner_in.at[step, 2], 1, -1),
            send(cell_face.at[step, 0, 0], cell_corner_in.at[step, 3], -1, -1),
        ]

    def finish_cells(step, copies):
        for copy in copies:
            copy.wait()
        start = pl.multiple_of(line * ROWS_Y, ROWS_Y)
        around = (lax.rem(start + lines * ROWS_Y - 1, lines * ROWS_Y), lax.rem(start + ROWS_Y, lines * ROWS_Y))
        for z in range(z_depth):
            rows = slice(z * ROWS_Y, (z + 1) * ROWS_Y)
            cell_post[0, rows, :] = jnp.where(
                first, inflow_rows[z, pl.ds(start, ROWS_Y), :], cell_edge_in[step, 0, rows, :])
            for way in range(2):
                cell_sides[way, 0, z : z + 1, :] = jnp.where(
                    first, inflow_rows[z, pl.ds(around[way], 1), :], cell_corner_in[step, 2 * way, z : z + 1, :])
        cell_post[end] = jnp.where(last, cell_post[rows_x], cell_edge_in[step, 1])
        for way in range(2):
            cell_sides[way, 1:end] = cell_face_in[step, way]
            cell_sides[way, end] = jnp.where(
                last, cell_face_in[step, way, rows_x - 1], cell_corner_in[step, 2 * way + 1])

    def send_columns(step, part):
        stride = pairs * QS * ROWS_Y
        flat = post.reshape(rows_x * stride, LANES)
        here = pl.ds(part * half, half)
        copies = []
        for pair in range(pairs):
            for ex in range(3):
                for ez in range(3):
                    for way, q, y in ((1, ex * 9 + 6 + ez, ROWS_Y - 1), (0, ex * 9 + ez, 0)):
                        from_row = part * half * stride + (pair * QS + q) * ROWS_Y + y
                        face[step, way, ex * 3 + ez, pair, part * half : (part + 1) * half, :] = flat[
                            pl.ds(from_row, half, stride=stride), :]
        copies.append(send(face.at[step, 1, :, :, here], face_in.at[step, 0, :, :, here], 0, 1))
        copies.append(send(face.at[step, 0, :, :, here], face_in.at[step, 1, :, :, here], 0, -1))
        dx = 1 if part else -1
        x = rows_x - 1 if part else 0
        for pair in range(pairs):
            for j in range(9):
                q = (18 if part else 0) + j
                edge[step, part, j, pair] = post[x, pair, q * ROWS_Y : (q + 1) * ROWS_Y, :]
            for i in range(3):
                r, j = i * pairs + pair, (6 if part else 0) + i
                for way in range(2):
                    corner[step, part, way, r : r + 1, :] = face[step, way, j, pair, x : x + 1, :]
        for way in range(2):
            corner[step, part, way, 3 * pairs :, :] = jnp.zeros((corner.shape[3] - 3 * pairs, LANES), jnp.float32)
        copies.append(send(edge.at[step, part], edge_in.at[step, 1 - part], dx, 0))
        for way in range(2):
            target = corner_in.at[step, 2 * (1 - way) + 1 - part]
            copies.append(send(corner.at[step, part, way], target, dx, 1 if way else -1))
        return copies

    def finish_columns(step, copies):
        for copy in copies:
            copy.wait()
        for pair in range(pairs):
            lanes = slice(pair * LANES, (pair + 1) * LANES)
            for j in range(9):
                own = post[rows_x - 1, pair, j * ROWS_Y : (j + 1) * ROWS_Y, :]
                x_rows[0, j, pair] = jnp.where(first, sens_rows[1, j, :, lanes], edge_in[step, 0, j, pair])
                x_rows[1, j, pair] = jnp.where(last, own, edge_in[step, 1, j, pair])
                for way in range(2):
                    sides[way, j, pair, 1:end] = face_in[step, way, j, pair]
            for way, take in ((0, 6), (1, 0)):
                y = ROWS_Y - 1 if way == 0 else 0
                for i in range(3):
                    r, k = i * pairs + pair, take + i
                    sides[way, 6 + i, pair, 0:1] = jnp.where(
                        first, sens_rows[2 * way, k, y : y + 1, lanes], corner_in[step, 2 * way, r : r + 1, :])
                    sides[way, i, pair, end : end + 1] = jnp.where(
                        last, face_in[step, way, i, pair, rows_x - 1 :, :], corner_in[step, 2 * way + 1, r : r + 1, :])

    inner = [(y, pair) for y in range(1, ROWS_Y - 1) for pair in range(pairs)]
    outer = [(y, pair) for y in (0, ROWS_Y - 1) for pair in range(pairs)]

    def outer_row(x, carry):
        move_columns(x, outer, jac, state, post)
        return carry

    def first_outer_row(x, carry):
        for pair in range(pairs):
            load(x, pair).wait()
        return outer_row(x, carry)

    def inner_row(x, carry):
        move_columns(x, inner, jac, state, post)
        return carry

    def keep_cells(x, z, value):
        cells[x, z * ROWS_Y : (z + 1) * ROWS_Y, :] = value

    def write_cells(x, z, value):
        primal_out[x, z * ROWS_Y : (z + 1) * ROWS_Y, :] = value[:, :27]

    def keep_columns(x, q, parts):
        for pair in range(pairs):
            state[x, pair, q * ROWS_Y : (q + 1) * ROWS_Y, :] = parts[pair]

    primal_collide(cells, cell_post, slope_one, slope_two, biases, lift, mix, drop)
    turning[...] = jnp.zeros(turning.shape, jnp.float32)
    size_y = inflow.shape[2]
    for z in range(z_depth):
        for from_y in range(0, size_y, LANES):
            many = min(LANES, size_y - from_y)
            turning[18:27, 0:many] = inflow[:, z, from_y : from_y + many]
            inflow_rows[z, from_y : from_y + LANES, :] = jnp.transpose(turning[...])
    for copy in sens_copies:
        copy.wait()

    column_copies = []
    for step in range(STEPS):
        earlier, column_copies = column_copies, []
        for part in range(2):
            jacobians(part * half, (part + 1) * half, jac, slope_one, slope_two, w_out, mid, pull)
            if step == 0 and part == 0:
                pl.semaphore_wait(barrier, peers - 1)
                cell_copies = send_cells(0)
            if step and part == 0:
                finish_columns(step - 1, earlier)
                stream_rows(post, x_rows, sides, keep_columns)
            lax.fori_loop(part * half, (part + 1) * half, outer_row if step else first_outer_row, 0, unroll=2)
            inner_row((rows_x - 1) * part, 0)
            column_copies += send_columns(step, part)
        lax.fori_loop(1, rows_x - 1, inner_row, 0)
        finish_cells(step, cell_copies)
        if step + 1 < STEPS:
            primal_stream(cell_post, cell_sides, mirror, keep_cells, z_depth)
            primal_collide(cells, cell_post, slope_one, slope_two, biases, lift, mix, drop)
            cell_copies = send_cells(step + 1)
        else:
            primal_stream(cell_post, cell_sides, mirror, write_cells, z_depth)

    sums = {}

    def write(x, q, parts):
        keep_columns(x, q, parts)
        for pair in range(pairs):
            if q == 0:
                sums[pair] = [None] * 4
            held = sums[pair]
            for m, factor in enumerate((1,) + LATTICE[q]):
                if factor == 0:
                    continue
                if held[m] is None:
                    held[m] = parts[pair] if factor == 1 else -parts[pair]
                else:
                    held[m] = held[m] + parts[pair] if factor == 1 else held[m] - parts[pair]
            if q == 26:
                for m in range(4):
                    observed[m, pair, pl.ds(pl.multiple_of(x * ROWS_Y, ROWS_Y), ROWS_Y), :] = held[m]

    finish_columns(STEPS - 1, column_copies)
    stream_rows(post, x_rows, sides, write)

    slots = probe_cells.shape[0]
    left = lane_iota(1) < LANES // 2

    def probe(peer, rows_out, place_out):
        for slot in range(slots):
            cell = jnp.clip(probe_cells[slot, peer], 0, observed.shape[2] * z_depth - 1)
            place, z = cell // z_depth, cell % z_depth
            pair, odd = z // 2, z % 2
            live = slot < probe_counts[0, peer]
            rows = [observed[m, pair, pl.ds(place, 1), :] for m in range(4)]
            turned = [pltpu.roll(r, LANES // 2, 1) for r in rows]
            for m in (0, 2):
                low = jnp.where(odd == 1, turned[m], rows[m])
                high = jnp.where(odd == 1, rows[m + 1], turned[m + 1])
                value = jnp.where(left, low, high)
                rows_out[place_out, slot : slot + 1, m * 64 : m * 64 + LANES] = jnp.where(live, value, 0.0)

    def share(other):
        return pltpu.make_async_remote_copy(
            src_ref=jac_rows.at[other], dst_ref=jac_in.at[me], send_sem=jac_send_sem.at[other],
            recv_sem=jac_recv_sem.at[me], device_id=(other // lines, lax.rem(other, lines)),
            device_id_type=pl.DeviceIdType.MESH,
        )

    def take(other):
        return pltpu.make_async_remote_copy(
            src_ref=jac_rows.at[other], dst_ref=jac_in.at[other], send_sem=jac_send_sem.at[other],
            recv_sem=jac_recv_sem.at[other], device_id=(other // lines, lax.rem(other, lines)),
            device_id_type=pl.DeviceIdType.MESH,
        )

    def start_share(i, carry):
        other = lax.rem(me + i, peers)
        probe(other, jac_rows, other)
        share(other).start()
        return carry

    def end_share(i, carry):
        take(lax.rem(me + i, peers)).wait()
        return carry

    lax.fori_loop(1, peers, start_share, 0)
    probe(me, jac_in, me)
    lax.fori_loop(1, peers, end_share, 0)
    jac_out[...] = jac_in[...]


def hand_out(primal, jac, tangent, primal_out, jac_out, tangent_out, sem, column_sem):
    rows_x, pairs = tangent.shape[0], tangent.shape[1]
    boxes = tangent.reshape(rows_x, pairs, QS, ROWS_Y, LANES)

    def store(x, pair):
        return pltpu.make_async_copy(
            boxes.at[x, pair, pl.ds(0, 27)], tangent_out.at[:, x, :, pl.ds(pair * LANES, LANES)], column_sem.at[x, pair])

    def start_store(x, carry):
        for pair in range(pairs):
            store(x, pair).start()
        return carry

    def end_store(x, carry):
        for pair in range(pairs):
            store(x, pair).wait()
        return carry

    small = [pltpu.make_async_copy(primal, primal_out, sem.at[0]), pltpu.make_async_copy(jac, jac_out, sem.at[1])]
    lax.fori_loop(0, rows_x, start_store, 0)
    for copy in small:
        copy.start()
    for copy in small:
        copy.wait()
    lax.fori_loop(0, rows_x, end_store, 0)


def shape(*dims):
    return jax.ShapeDtypeStruct(dims, jnp.float32)


def on_device(primal_pops, tangent_pops, inflow_pops, inflow_sens, w_in, b_in, w_mid, b_mid, w_out, b_out,
              probe_cells, probe_counts):
    rows_x, rows_y, z_depth = primal_pops.shape[1:]
    width = tangent_pops.shape[3]
    pairs = width // LANES
    plane = z_depth * rows_y
    size_y = inflow_pops.shape[1]
    padded_y = -(-size_y // LANES) * LANES
    peers, slots = probe_cells.shape[1:]
    columns = 4 * width // z_depth
    corner_rows = -(-3 * pairs // 8) * 8

    cells = jnp.transpose(primal_pops, (1, 3, 2, 0)).reshape(rows_x, plane, 27)
    inflow = jnp.transpose(inflow_pops, (0, 2, 1))
    where_probes = jnp.transpose(probe_cells[0], (1, 0))

    def room(*dims, kind=jnp.float32):
        return pltpu.VMEM(dims, kind)

    def weight(n):
        return room(2 * LANES, n, kind=jnp.bfloat16)

    dma = pltpu.SemaphoreType.DMA
    scratch = [
        room(rows_x, plane, LANES),
        weight(2 * LANES), weight(2 * LANES), weight(2 * LANES), weight(2 * LANES), weight(LANES),
        room(rows_x, plane, LANES),
        room(rows_x, plane, LANES),
        room(LANES, LANES),
        room(z_depth, padded_y, LANES),
        room(rows_x + 2, plane, LANES),
        room(2, rows_x + 2, 8, LANES),
        room(2, rows_x, rows_y, LANES),
        room(STEPS, 2, plane, LANES),
        room(STEPS, 2, rows_x, 8, LANES),
        room(STEPS, 2, plane, LANES),
        room(STEPS, 2, rows_x, 8, LANES),
        room(STEPS, 4, 8, LANES),
        room(rows_x, z_depth, QS * rows_y, LANES),
        room(rows_x, pairs, QS * rows_y, LANES),
        room(3, 9, rows_y, width),
        room(2, 9, pairs, rows_y, LANES),
        room(2, 9, pairs, rows_x + 8, LANES),
        room(STEPS, 2, 9, pairs, rows_y, LANES),
        room(STEPS, 2, 9, pairs, rows_x, LANES),
        room(STEPS, 2, 2, corner_rows, LANES),
        room(STEPS, 2, 9, pairs, rows_y, LANES),
        room(STEPS, 2, 9, pairs, rows_x, LANES),
        room(STEPS, 4, corner_rows, LANES),
        room(4, pairs, rows_x * rows_y, LANES),
        room(peers, slots, columns),
        room(peers, slots, columns),
        dma((rows_x, pairs)),
        dma((3,)),
        dma((18 * STEPS,)),
        dma((18 * STEPS,)),
        dma((peers,)),
        dma((peers,)),
    ]
    smem = pl.BlockSpec(memory_space=pltpu.SMEM)
    vmem = pl.BlockSpec(memory_space=pltpu.VMEM)
    left_out = pl.BlockSpec(memory_space=pl.ANY)
    held = pl.pallas_call(
        functools.partial(kernel, z_depth),
        out_shape=(
            room(rows_x, plane, 27), room(peers, slots, columns), room(rows_x, pairs, QS * rows_y, LANES)),
        in_specs=[smem, smem] + [vmem] * 8 + [left_out] * 2,
        out_specs=(vmem,) * 3,
        scratch_shapes=scratch,
        compiler_params=pltpu.CompilerParams(vmem_limit_bytes=VMEM_LIMIT, collective_id=1, has_side_effects=True),
        name="slab",
    )(where_probes, probe_counts, cells, inflow, w_in.T, b_in[None], w_mid, b_mid[None], w_out, b_out[None],
      tangent_pops, inflow_sens)
    primal, jac, tangent = pl.pallas_call(
        hand_out,
        out_shape=(shape(rows_x, plane, 27), shape(peers, slots, columns), shape(*tangent_pops.shape)),
        in_specs=[vmem] * 3,
        out_specs=(left_out,) * 3,
        scratch_shapes=[dma((2,)), dma((rows_x, pairs))],
        compiler_params=pltpu.CompilerParams(vmem_limit_bytes=1024 * 1024),
        name="hand_out",
    )(*held)
    primal = jnp.transpose(primal.reshape(rows_x, z_depth, rows_y, 27), (3, 0, 2, 1))
    return primal, tangent, jac[None]


def solution(mesh):
    both = P(("gx", "gy"))
    split_xy = P(None, "gx", "gy", None)
    return jax.shard_map(
        on_device,
        mesh=mesh,
        in_specs=(split_xy, split_xy) + (P(),) * 8 + (both, both),
        out_specs=(split_xy, split_xy, both),
        check_vma=False,
    )
```

```python
import functools

import jax
import jax.numpy as jnp
from jax import lax
from jax.experimental import pallas as pl
from jax.experimental.pallas import tpu as pltpu
from jax.sharding import PartitionSpec as P

STEPS = 2
QS = 32
LANES = 128
ROWS_Y = 8
CHUNK = 9
VMEM_LIMIT = 54 * 1024 * 1024
LATTICE = [(q // 9 - 1, q // 3 % 3 - 1, q % 3 - 1) for q in range(27)]


def split(value):
    high = value.astype(jnp.bfloat16)
    low = (value - high.astype(jnp.float32)).astype(jnp.bfloat16)
    return high, low


def dot(a, b):
    return jnp.dot(a, b, preferred_element_type=jnp.float32)


def lane_iota(rows):
    return lax.broadcasted_iota(jnp.int32, (rows, LANES), 1)


def sublane_iota(rows):
    return lax.broadcasted_iota(jnp.int32, (rows, LANES), 0)


def fill(value, rows, columns):
    if value.shape[1] < columns:
        value = jnp.concatenate([value, jnp.zeros((value.shape[0], columns - value.shape[1]), value.dtype)], axis=1)
    if value.shape[0] < rows:
        value = jnp.concatenate([value, jnp.zeros((rows - value.shape[0], columns), value.dtype)], axis=0)
    return value


def three_products(weight):
    high, low = split(weight)
    return jnp.concatenate(
        [jnp.concatenate([high, low], axis=1), jnp.concatenate([high, jnp.zeros_like(low)], axis=1)], axis=0
    )


def times(value, weight):
    high, low = split(value)
    both = dot(jnp.concatenate([high, low], axis=1), weight[...])
    return both[:, :LANES] + both[:, LANES:]


def make_weights(w_in_t, w_mid, w_out, lift, mix, drop, mid, pull):
    turned_in = fill(w_in_t[...], LANES, LANES)
    lift[...] = three_products(turned_in)
    mix[...] = three_products(jnp.transpose(w_mid[...]))
    drop[...] = three_products(jnp.transpose(fill(w_out[...], LANES, LANES)))
    mid[...] = three_products(w_mid[...])
    top = turned_in[:QS]
    high = top.astype(jnp.bfloat16).astype(jnp.float32)
    wide = jnp.transpose(jnp.concatenate([high, top - high, high, high], axis=0))
    lane = lane_iota(LANES)
    only_high = jnp.where((lane >= QS) & (lane < 2 * QS), 0.0, wide)
    pull[...] = jnp.concatenate([wide, only_high], axis=0).astype(jnp.bfloat16)


def primal_collide(cells, post, slope_one, slope_two, biases, lift, mix, drop):
    rows_x, plane = cells.shape[0], cells.shape[1]
    bias_in, bias_mid, bias_out = biases
    block = 4

    def rows(i, carry):
        at = pl.multiple_of(i * block, block)
        cell = cells[pl.ds(at, block)].reshape(block * plane, LANES)
        act_one = jnp.tanh(times(cell, lift) + bias_in)
        act_two = jnp.tanh(times(act_one, mix) + bias_mid)
        after = cell + times(act_two, drop) + bias_out
        slope_one[pl.ds(at, block)] = (1.0 - act_one * act_one).reshape(block, plane, LANES)
        slope_two[pl.ds(at, block)] = (1.0 - act_two * act_two).reshape(block, plane, LANES)
        post[pl.ds(at + 1, block)] = after.reshape(block, plane, LANES)
        return carry

    lax.fori_loop(0, rows_x // block, rows, 0)


def primal_stream(post, sides, mirror, write, z_depth):
    rows_x = post.shape[0] - 2
    lane, at_y = lane_iota(ROWS_Y), sublane_iota(ROWS_Y)
    plus_x, minus_x = (lane >= 18) & (lane < 27), lane < 9
    step_y, step_z = lane // 3 % 3, lane % 3
    turn = jnp.where((lane_iota(LANES) + sublane_iota(LANES) == 26), 1.0, 0.0).astype(jnp.bfloat16)
    turn = jnp.concatenate([turn, turn], axis=0)
    for end, z in ((0, 0), (1, z_depth - 1)):
        wall = post[1 : rows_x + 1, z * ROWS_Y : (z + 1) * ROWS_Y, :].reshape(rows_x * ROWS_Y, LANES)
        high, middle = split(wall)
        rest = (wall - high.astype(jnp.float32) - middle.astype(jnp.float32)).astype(jnp.bfloat16)
        turned = dot(jnp.concatenate([high, middle], axis=1), turn) + dot(rest, turn[:LANES])
        mirror[end] = turned.reshape(rows_x, ROWS_Y, LANES)

    def row(x, carry):
        def from_x(take):
            return jnp.where(plus_x, take(x), jnp.where(minus_x, take(x + 2), take(x + 1)))

        low = from_x(lambda i: sides[0, i])
        high = from_x(lambda i: sides[1, i])
        planes = []
        for z in range(z_depth):
            own = from_x(lambda i: post[i, z * ROWS_Y : (z + 1) * ROWS_Y, :])
            up = jnp.where(at_y == 0, low[z : z + 1], pltpu.roll(own, 1, 0))
            down = jnp.where(at_y == ROWS_Y - 1, high[z : z + 1], pltpu.roll(own, ROWS_Y - 1, 0))
            planes.append(jnp.where(step_y == 2, up, jnp.where(step_y == 0, down, own)))
        for z in range(z_depth):
            below = planes[z - 1] if z else mirror[0, x]
            above = planes[z + 1] if z + 1 < z_depth else mirror[1, x]
            write(x, z, jnp.where(step_z == 2, below, jnp.where(step_z == 0, above, planes[z])))
        return carry

    lax.fori_loop(0, rows_x, row, 0)


def jacobians(from_x, to_x, jac, slope_one, slope_two, w_out, mid, pull):
    plane, z_depth = slope_one.shape[1], jac.shape[1]

    def row(x, carry):
        one, two = slope_one[x], slope_two[x]

        def finish(first, high, low):
            ready = dot(jnp.concatenate([high, low], axis=1), pull[...])
            for i in range(CHUNK):
                for z in range(z_depth):
                    at = i * plane + z * ROWS_Y
                    jac[x, z, (first + i) * ROWS_Y : (first + i + 1) * ROWS_Y, :] = ready[at : at + ROWS_Y]

        waiting = None
        for first in range(0, 27, CHUNK):
            outer = (w_out[first : first + CHUNK, :][:, None, :] * two[None]).reshape(CHUNK * plane, LANES)
            high, low = split(outer)
            both = dot(jnp.concatenate([high, low], axis=1), mid[...])
            if waiting is not None:
                finish(*waiting)
            middle = both[:, :LANES] + both[:, LANES:]
            middle = (middle.reshape(CHUNK, plane, LANES) * one[None]).reshape(CHUNK * plane, LANES)
            waiting = (first, *split(middle))
        finish(*waiting)
        return carry

    lax.fori_loop(from_x, to_x, row, 0, unroll=4)


def move_columns(x, columns, jac, state, post):
    lane = lane_iota(QS)
    left, low_part = lane < LANES // 2, (lane >= 2 * QS) & (lane < 3 * QS)

    def cell_rows(y, z):
        rows = jac[x, z, pl.ds(y, QS, stride=ROWS_Y), :]
        high = rows.astype(jnp.bfloat16).astype(jnp.float32)
        return jnp.where(low_part, rows - high, rows).astype(jnp.bfloat16)

    for y, pair in columns:
        cell = state[x, pair, pl.ds(y, QS, stride=ROWS_Y), :]
        high, low = split(cell)
        none = jnp.zeros_like(high)
        parts = []
        for keep in (lambda v: jnp.where(left, v, none), lambda v: jnp.where(left, none, v)):
            parts += [keep(high)] * 3 + [keep(low)]
        rows = jnp.concatenate([cell_rows(y, 2 * pair), cell_rows(y, 2 * pair + 1)], axis=1)
        post[x, pair, pl.ds(y, QS, stride=ROWS_Y), :] = cell + dot(rows, jnp.concatenate(parts, axis=0))


def stream_rows(before, x_rows, sides, write):
    rows_x, pairs = before.shape[0], before.shape[1]
    rows_y = ROWS_Y
    lane = lane_iota(rows_y)
    left = lane < LANES // 2
    at_y = lax.broadcasted_iota(jnp.int32, (rows_y, LANES), 0)
    def one_row(x, edge):
        for q, (ex, ey, ez) in enumerate(LATTICE):
            parts = []
            for pair in range(pairs):
                if edge == -1 and ex == 1:
                    value = x_rows[0, q - 18, pair]
                elif edge == 1 and ex == -1:
                    value = x_rows[1, q, pair]
                else:
                    value = before[x - ex, pair, q * rows_y : (q + 1) * rows_y, :]
                if ey != 0:
                    j = (ex + 1) * 3 + ez + 1
                    side = sides[0 if ey == 1 else 1, j, pair, pl.ds(x - ex + 1, 1), :]
                    if ey == 1:
                        value = jnp.where(at_y == 0, side, pltpu.roll(value, 1, 0))
                    else:
                        value = jnp.where(at_y == rows_y - 1, side, pltpu.roll(value, rows_y - 1, 0))
                parts.append(value)
            if ez != 0:
                turned = [pltpu.roll(part, LANES // 2, 1) for part in parts]
                mirror = 26 - q
                if ez == 1:
                    wall = before[x, 0, mirror * rows_y : (mirror + 1) * rows_y, :]
                    parts = [jnp.where(left, turned[p - 1] if p else wall, turned[p]) for p in range(pairs)]
                else:
                    wall = before[x, pairs - 1, mirror * rows_y : (mirror + 1) * rows_y, :]
                    parts = [jnp.where(left, turned[p], turned[p + 1] if p + 1 < pairs else wall) for p in range(pairs)]
            write(x, q, parts)

    one_row(0, -1)

    def inner(x, carry):
        one_row(x, 0)
        return carry

    lax.fori_loop(1, rows_x - 1, inner, 0)
    one_row(rows_x - 1, 1)


def kernel(z_depth, probe_cells, probe_counts, cells_in, inflow, w_in_t, b_in, w_mid, b_mid, w_out, b_out,
           tangent, sens, primal_out, jac_out, columns_out, *scratch):
    (cells, lift, mix, drop, mid, pull, slope_one, slope_two, turning, inflow_rows, cell_post, cell_sides, mirror,
     cell_edge, cell_face, cell_edge_in, cell_face_in, cell_corner_in, jac, state, post, sens_rows, x_rows, sides,
     edge, face, corner, edge_in, face_in, corner_in, observed, jac_rows, jac_in,
     load_sem, sens_sem, send_sem, recv_sem, jac_send_sem, jac_recv_sem) = scratch
    rows_x, pairs, plane = state.shape[0], state.shape[1], cells.shape[1]
    column, columns_x = lax.axis_index("gx"), lax.axis_size("gx")
    line, lines = lax.axis_index("gy"), lax.axis_size("gy")
    me, peers = column * lines + line, columns_x * lines
    first, last = column == 0, column == columns_x - 1
    end, half = rows_x + 1, rows_x // 2

    def at(dx, dy):
        return (lax.rem(column + dx + columns_x, columns_x), lax.rem(line + dy + lines, lines))

    barrier = pltpu.get_barrier_semaphore()

    def greet(i, carry):
        other = lax.rem(me + i, peers)
        pl.semaphore_signal(barrier, inc=1, device_id=(other // lines, lax.rem(other, lines)),
                            device_id_type=pl.DeviceIdType.MESH)
        return carry

    lax.fori_loop(1, peers, greet, 0)

    boxes = state.reshape(rows_x, pairs, QS, ROWS_Y, LANES)

    def load(x, pair):
        return pltpu.make_async_copy(
            tangent.at[:, x, :, pl.ds(pair * LANES, LANES)], boxes.at[x, pair, pl.ds(0, 27)], load_sem.at[x, pair])

    def start_load(x, carry):
        for pair in range(pairs):
            load(x, pair).start()
        return carry

    lax.fori_loop(0, rows_x, start_load, 0)
    sens_copies = []
    for i in range(3):
        from_y = pl.multiple_of(lax.rem(line + i - 1 + lines, lines) * ROWS_Y, ROWS_Y)
        copy = pltpu.make_async_copy(sens.at[:, pl.ds(from_y, ROWS_Y), :], sens_rows.at[i], sens_sem.at[i])
        copy.start()
        sens_copies.append(copy)

    counter = [0]

    def send(source, target, dx, dy):
        i = counter[0]
        counter[0] += 1
        copy = pltpu.make_async_remote_copy(
            src_ref=source, dst_ref=target, send_sem=send_sem.at[i], recv_sem=recv_sem.at[i],
            device_id=at(dx, dy), device_id_type=pl.DeviceIdType.MESH,
        )
        copy.start()
        return copy

    make_weights(w_in_t, w_mid, w_out, lift, mix, drop, mid, pull)
    biases = (b_in[...], b_mid[...], fill(b_out[...], 1, LANES))
    cells[...] = jnp.zeros(cells.shape, jnp.float32)
    cells[:, :, 0:27] = cells_in[...]

    def clear(x, carry):
        for z in range(z_depth):
            jac[x, z, 27 * ROWS_Y :, :] = jnp.zeros(((QS - 27) * ROWS_Y, LANES), jnp.float32)
        for pair in range(pairs):
            state[x, pair, 27 * ROWS_Y :, :] = jnp.zeros(((QS - 27) * ROWS_Y, LANES), jnp.float32)
        return carry

    lax.fori_loop(0, rows_x, clear, 0)

    def send_cells(step):
        for x in range(rows_x):
            for way, y in ((0, 0), (1, ROWS_Y - 1)):
                for z in range(z_depth):
                    cell_face[step, way, x, z : z + 1, :] = cell_post[x + 1, z * ROWS_Y + y : z * ROWS_Y + y + 1, :]
                cell_face[step, way, x, z_depth:, :] = jnp.zeros((8 - z_depth, LANES), jnp.float32)
        cell_edge[step, 0] = cell_post[1]
        cell_edge[step, 1] = cell_post[rows_x]
        return [
            send(cell_edge.at[step, 1], cell_edge_in.at[step, 0], 1, 0),
            send(cell_edge.at[step, 0], cell_edge_in.at[step, 1], -1, 0),
            send(cell_face.at[step, 1], cell_face_in.at[step, 0], 0, 1),
            send(cell_face.at[step, 0], cell_face_in.at[step, 1], 0, -1),
            send(cell_face.at[step, 1, rows_x - 1], cell_corner_in.at[step, 0], 1, 1),
            send(cell_face.at[step, 1, 0], cell_corner_in.at[step, 1], -1, 1),
            send(cell_face.at[step, 0, rows_x - 1], cell_corner_in.at[step, 2], 1, -1),
            send(cell_face.at[step, 0, 0], cell_corner_in.at[step, 3], -1, -1),
        ]

    def finish_cells(step, copies):
        for copy in copies:
            copy.wait()
        start = pl.multiple_of(line * ROWS_Y, ROWS_Y)
        around = (lax.rem(start + lines * ROWS_Y - 1, lines * ROWS_Y), lax.rem(start + ROWS_Y, lines * ROWS_Y))
        for z in range(z_depth):
            rows = slice(z * ROWS_Y, (z + 1) * ROWS_Y)
            cell_post[0, rows, :] = jnp.where(
                first, inflow_rows[z, pl.ds(start, ROWS_Y), :], cell_edge_in[step, 0, rows, :])
            for way in range(2):
                cell_sides[way, 0, z : z + 1, :] = jnp.where(
                    first, inflow_rows[z, pl.ds(around[way], 1), :], cell_corner_in[step, 2 * way, z : z + 1, :])
        cell_post[end] = jnp.where(last, cell_post[rows_x], cell_edge_in[step, 1])
        for way in range(2):
            cell_sides[way, 1:end] = cell_face_in[step, way]
            cell_sides[way, end] = jnp.where(
                last, cell_face_in[step, way, rows_x - 1], cell_corner_in[step, 2 * way + 1])

    def send_columns(step, part):
        stride = pairs * QS * ROWS_Y
        flat = post.reshape(rows_x * stride, LANES)
        here = pl.ds(part * half, half)
        copies = []
        for pair in range(pairs):
            for ex in range(3):
                for ez in range(3):
                    for way, q, y in ((1, ex * 9 + 6 + ez, ROWS_Y - 1), (0, ex * 9 + ez, 0)):
                        from_row = part * half * stride + (pair * QS + q) * ROWS_Y + y
                        face[step, way, ex * 3 + ez, pair, part * half : (part + 1) * half, :] = flat[
                            pl.ds(from_row, half, stride=stride), :]
        copies.append(send(face.at[step, 1, :, :, here], face_in.at[step, 0, :, :, here], 0, 1))
        copies.append(send(face.at[step, 0, :, :, here], face_in.at[step, 1, :, :, here], 0, -1))
        dx = 1 if part else -1
        x = rows_x - 1 if part else 0
        for pair in range(pairs):
            for j in range(9):
                q = (18 if part else 0) + j
                edge[step, part, j, pair] = post[x, pair, q * ROWS_Y : (q + 1) * ROWS_Y, :]
            for i in range(3):
                r, j = i * pairs + pair, (6 if part else 0) + i
                for way in range(2):
                    corner[step, part, way, r : r + 1, :] = face[step, way, j, pair, x : x + 1, :]
        for way in range(2):
            corner[step, part, way, 3 * pairs :, :] = jnp.zeros((corner.shape[3] - 3 * pairs, LANES), jnp.float32)
        copies.append(send(edge.at[step, part], edge_in.at[step, 1 - part], dx, 0))
        for way in range(2):
            target = corner_in.at[step, 2 * (1 - way) + 1 - part]
            copies.append(send(corner.at[step, part, way], target, dx, 1 if way else -1))
        return copies

    def finish_columns(step, copies):
        for copy in copies:
            copy.wait()
        for pair in range(pairs):
            lanes = slice(pair * LANES, (pair + 1) * LANES)
            for j in range(9):
                own = post[rows_x - 1, pair, j * ROWS_Y : (j + 1) * ROWS_Y, :]
                x_rows[0, j, pair] = jnp.where(first, sens_rows[1, j, :, lanes], edge_in[step, 0, j, pair])
                x_rows[1, j, pair] = jnp.where(last, own, edge_in[step, 1, j, pair])
                for way in range(2):
                    sides[way, j, pair, 1:end] = face_in[step, way, j, pair]
            for way, take in ((0, 6), (1, 0)):
                y = ROWS_Y - 1 if way == 0 else 0
                for i in range(3):
                    r, k = i * pairs + pair, take + i
                    sides[way, 6 + i, pair, 0:1] = jnp.where(
                        first, sens_rows[2 * way, k, y : y + 1, lanes], corner_in[step, 2 * way, r : r + 1, :])
                    sides[way, i, pair, end : end + 1] = jnp.where(
                        last, face_in[step, way, i, pair, rows_x - 1 :, :], corner_in[step, 2 * way + 1, r : r + 1, :])

    inner = [(y, pair) for y in range(1, ROWS_Y - 1) for pair in range(pairs)]
    outer = [(y, pair) for y in (0, ROWS_Y - 1) for pair in range(pairs)]

    def outer_row(x, carry):
        move_columns(x, outer, jac, state, post)
        return carry

    def first_outer_row(x, carry):
        for pair in range(pairs):
            load(x, pair).wait()
        return outer_row(x, carry)

    def inner_row(x, carry):
        move_columns(x, inner, jac, state, post)
        return carry

    def keep_cells(x, z, value):
        cells[x, z * ROWS_Y : (z + 1) * ROWS_Y, :] = value

    def write_cells(x, z, value):
        primal_out[x, z * ROWS_Y : (z + 1) * ROWS_Y, :] = value[:, :27]

    def keep_columns(x, q, parts):
        for pair in range(pairs):
            state[x, pair, q * ROWS_Y : (q + 1) * ROWS_Y, :] = parts[pair]

    primal_collide(cells, cell_post, slope_one, slope_two, biases, lift, mix, drop)
    turning[...] = jnp.zeros(turning.shape, jnp.float32)
    size_y = inflow.shape[2]
    for z in range(z_depth):
        for from_y in range(0, size_y, LANES):
            many = min(LANES, size_y - from_y)
            turning[18:27, 0:many] = inflow[:, z, from_y : from_y + many]
            inflow_rows[z, from_y : from_y + LANES, :] = jnp.transpose(turning[...])
    for copy in sens_copies:
        copy.wait()

    column_copies = []
    for step in range(STEPS):
        earlier, column_copies = column_copies, []
        for part in range(2):
            jacobians(part * half, (part + 1) * half, jac, slope_one, slope_two, w_out, mid, pull)
            if step == 0 and part == 0:
                pl.semaphore_wait(barrier, peers - 1)
                cell_copies = send_cells(0)
            if step and part == 0:
                finish_columns(step - 1, earlier)
                stream_rows(post, x_rows, sides, keep_columns)
            lax.fori_loop(part * half, (part + 1) * half, outer_row if step else first_outer_row, 0, unroll=4)
            inner_row((rows_x - 1) * part, 0)
            column_copies += send_columns(step, part)
        lax.fori_loop(1, rows_x - 1, inner_row, 0, unroll=2)
        finish_cells(step, cell_copies)
        if step + 1 < STEPS:
            primal_stream(cell_post, cell_sides, mirror, keep_cells, z_depth)
            primal_collide(cells, cell_post, slope_one, slope_two, biases, lift, mix, drop)
            cell_copies = send_cells(step + 1)
        else:
            primal_stream(cell_post, cell_sides, mirror, write_cells, z_depth)

    sums = {}
    left = lane_iota(ROWS_Y) < LANES // 2

    def write(x, q, parts):
        for pair in range(pairs):
            columns_out[q, x, :, pair * LANES : (pair + 1) * LANES] = parts[pair]
            if q == 0:
                sums[pair] = [None] * 4
            held = sums[pair]
            for m, factor in enumerate((1,) + LATTICE[q]):
                if factor == 0:
                    continue
                if held[m] is None:
                    held[m] = parts[pair] if factor == 1 else -parts[pair]
                else:
                    held[m] = held[m] + parts[pair] if factor == 1 else held[m] - parts[pair]
            if q == 26:
                here = pl.ds(pl.multiple_of(x * ROWS_Y, ROWS_Y), ROWS_Y)
                for m in (0, 2):
                    observed[m // 2, 2 * pair, here, :] = jnp.where(
                        left, held[m], pltpu.roll(held[m + 1], LANES // 2, 1))
                    observed[m // 2, 2 * pair + 1, here, :] = jnp.where(
                        left, pltpu.roll(held[m], LANES // 2, 1), held[m + 1])

    finish_columns(STEPS - 1, column_copies)
    stream_rows(post, x_rows, sides, write)

    slots = probe_cells.shape[0]

    def probe(peer, rows_out, place_out):
        for slot in range(slots):
            cell = jnp.clip(probe_cells[slot, peer], 0, observed.shape[2] * z_depth - 1)
            place, z = cell // z_depth, cell % z_depth
            live = slot < probe_counts[0, peer]
            for m in range(2):
                value = observed[m, z, pl.ds(place, 1), :]
                rows_out[place_out, slot : slot + 1, m * LANES : (m + 1) * LANES] = jnp.where(live, value, 0.0)

    def share(source, target, other):
        return pltpu.make_async_remote_copy(
            src_ref=source, dst_ref=target, send_sem=jac_send_sem, recv_sem=jac_recv_sem,
            device_id=(other // lines, lax.rem(other, lines)), device_id_type=pl.DeviceIdType.MESH,
        )

    def start_share(i, carry):
        other = lax.rem(me + i, peers)
        probe(other, jac_rows, other)
        share(jac_rows.at[other], jac_in.at[me], other).start()
        return carry

    lax.fori_loop(1, peers, start_share, 0, unroll=4)
    probe(me, jac_in, me)
    everyone = pl.ds(0, peers - 1)
    share(jac_rows.at[everyone], jac_in.at[everyone], lax.rem(me + 1, peers)).wait()
    jac_out[...] = jac_in[...]


def hand_out(primal, jac, tangent, primal_out, jac_out, tangent_out, sem):
    copies = []

    def start(source, target):
        copies.append(pltpu.make_async_copy(source, target, sem.at[len(copies)]))
        copies[-1].start()

    for q in range(0, 27, 3):
        start(tangent.at[pl.ds(q, 3)], tangent_out.at[pl.ds(q, 3)])
    start(primal, primal_out)
    start(jac, jac_out)
    for copy in copies:
        copy.wait()


def shape(*dims):
    return jax.ShapeDtypeStruct(dims, jnp.float32)


def on_device(primal_pops, tangent_pops, inflow_pops, inflow_sens, w_in, b_in, w_mid, b_mid, w_out, b_out,
              probe_cells, probe_counts):
    rows_x, rows_y, z_depth = primal_pops.shape[1:]
    width = tangent_pops.shape[3]
    pairs = width // LANES
    plane = z_depth * rows_y
    size_y = inflow_pops.shape[1]
    padded_y = -(-size_y // LANES) * LANES
    peers, slots = probe_cells.shape[1:]
    columns = 4 * width // z_depth
    corner_rows = -(-3 * pairs // 8) * 8

    cells = jnp.transpose(primal_pops, (1, 3, 2, 0)).reshape(rows_x, plane, 27)
    inflow = jnp.transpose(inflow_pops, (0, 2, 1))
    where_probes = jnp.transpose(probe_cells[0], (1, 0))

    def room(*dims, kind=jnp.float32):
        return pltpu.VMEM(dims, kind)

    def weight(n):
        return room(2 * LANES, n, kind=jnp.bfloat16)

    dma = pltpu.SemaphoreType.DMA
    scratch = [
        room(rows_x, plane, LANES),
        weight(2 * LANES), weight(2 * LANES), weight(2 * LANES), weight(2 * LANES), weight(LANES),
        room(rows_x, plane, LANES),
        room(rows_x, plane, LANES),
        room(LANES, LANES),
        room(z_depth, padded_y, LANES),
        room(rows_x + 2, plane, LANES),
        room(2, rows_x + 2, 8, LANES),
        room(2, rows_x, rows_y, LANES),
        room(STEPS, 2, plane, LANES),
        room(STEPS, 2, rows_x, 8, LANES),
        room(STEPS, 2, plane, LANES),
        room(STEPS, 2, rows_x, 8, LANES),
        room(STEPS, 4, 8, LANES),
        room(rows_x, z_depth, QS * rows_y, LANES),
        room(rows_x, pairs, QS * rows_y, LANES),
        room(rows_x, pairs, QS * rows_y, LANES),
        room(3, 9, rows_y, width),
        room(2, 9, pairs, rows_y, LANES),
        room(2, 9, pairs, rows_x + 8, LANES),
        room(STEPS, 2, 9, pairs, rows_y, LANES),
        room(STEPS, 2, 9, pairs, rows_x, LANES),
        room(STEPS, 2, 2, corner_rows, LANES),
        room(STEPS, 2, 9, pairs, rows_y, LANES),
        room(STEPS, 2, 9, pairs, rows_x, LANES),
        room(STEPS, 4, corner_rows, LANES),
        room(2, z_depth, rows_x * rows_y, LANES),
        room(peers, slots, columns),
        room(peers, slots, columns),
        dma((rows_x, pairs)),
        dma((3,)),
        dma((18 * STEPS,)),
        dma((18 * STEPS,)),
        dma,
        dma,
    ]
    smem = pl.BlockSpec(memory_space=pltpu.SMEM)
    vmem = pl.BlockSpec(memory_space=pltpu.VMEM)
    left_out = pl.BlockSpec(memory_space=pl.ANY)
    held = pl.pallas_call(
        functools.partial(kernel, z_depth),
        out_shape=(
            room(rows_x, plane, 27), room(peers, slots, columns), room(*tangent_pops.shape)),
        in_specs=[smem, smem] + [vmem] * 8 + [left_out] * 2,
        out_specs=(vmem,) * 3,
        scratch_shapes=scratch,
        compiler_params=pltpu.CompilerParams(vmem_limit_bytes=VMEM_LIMIT, collective_id=1, has_side_effects=True),
        name="slab",
    )(where_probes, probe_counts, cells, inflow, w_in.T, b_in[None], w_mid, b_mid[None], w_out, b_out[None],
      tangent_pops, inflow_sens)
    primal, jac, tangent = pl.pallas_call(
        hand_out,
        out_shape=(shape(rows_x, plane, 27), shape(peers, slots, columns), shape(*tangent_pops.shape)),
        in_specs=[vmem] * 3,
        out_specs=(left_out,) * 3,
        scratch_shapes=[dma((11,))],
        compiler_params=pltpu.CompilerParams(vmem_limit_bytes=1024 * 1024),
        name="hand_out",
    )(*held)
    primal = jnp.transpose(primal.reshape(rows_x, z_depth, rows_y, 27), (3, 0, 2, 1))
    return primal, tangent, jac[None]


def solution(mesh):
    both = P(("gx", "gy"))
    split_xy = P(None, "gx", "gy", None)
    return jax.shard_map(
        on_device,
        mesh=mesh,
        in_specs=(split_xy, split_xy) + (P(),) * 8 + (both, both),
        out_specs=(split_xy, split_xy, both),
        check_vma=False,
    )
```

```python
import functools

import jax
import jax.numpy as jnp
from jax import lax
from jax.experimental import pallas as pl
from jax.experimental.pallas import tpu as pltpu
from jax.sharding import PartitionSpec as P

STEPS = 2
QS = 32
LANES = 128
ROWS_Y = 8
CHUNK = 9
VMEM_LIMIT = 54 * 1024 * 1024
LATTICE = [(q // 9 - 1, q // 3 % 3 - 1, q % 3 - 1) for q in range(27)]


def split(value):
    high = value.astype(jnp.bfloat16)
    low = (value - high.astype(jnp.float32)).astype(jnp.bfloat16)
    return high, low


def dot(a, b):
    return jnp.dot(a, b, preferred_element_type=jnp.float32)


def lane_iota(rows):
    return lax.broadcasted_iota(jnp.int32, (rows, LANES), 1)


def sublane_iota(rows):
    return lax.broadcasted_iota(jnp.int32, (rows, LANES), 0)


def fill(value, rows, columns):
    if value.shape[1] < columns:
        value = jnp.concatenate([value, jnp.zeros((value.shape[0], columns - value.shape[1]), value.dtype)], axis=1)
    if value.shape[0] < rows:
        value = jnp.concatenate([value, jnp.zeros((rows - value.shape[0], columns), value.dtype)], axis=0)
    return value


def three_products(weight):
    high, low = split(weight)
    return jnp.concatenate(
        [jnp.concatenate([high, low], axis=1), jnp.concatenate([high, jnp.zeros_like(low)], axis=1)], axis=0
    )


def times(value, weight):
    high, low = split(value)
    both = dot(jnp.concatenate([high, low], axis=1), weight[...])
    return both[:, :LANES] + both[:, LANES:]


def make_weights(w_in_t, w_mid, w_out, lift, mix, drop, mid, pull):
    turned_in = fill(w_in_t[...], LANES, LANES)
    lift[...] = three_products(turned_in)
    mix[...] = three_products(jnp.transpose(w_mid[...]))
    drop[...] = three_products(jnp.transpose(fill(w_out[...], LANES, LANES)))
    mid[...] = three_products(w_mid[...])
    top = turned_in[:QS]
    high = top.astype(jnp.bfloat16).astype(jnp.float32)
    wide = jnp.transpose(jnp.concatenate([high, top - high, high, high], axis=0))
    lane = lane_iota(LANES)
    only_high = jnp.where((lane >= QS) & (lane < 2 * QS), 0.0, wide)
    pull[...] = jnp.concatenate([wide, only_high], axis=0).astype(jnp.bfloat16)


def primal_collide(cells, post, slope_one, slope_two, biases, lift, mix, drop):
    rows_x, plane = cells.shape[0], cells.shape[1]
    bias_in, bias_mid, bias_out = biases
    block = 4

    def rows(i, carry):
        at = pl.multiple_of(i * block, block)
        cell = cells[pl.ds(at, block)].reshape(block * plane, LANES)
        act_one = jnp.tanh(times(cell, lift) + bias_in)
        act_two = jnp.tanh(times(act_one, mix) + bias_mid)
        after = cell + times(act_two, drop) + bias_out
        slope_one[pl.ds(at, block)] = (1.0 - act_one * act_one).reshape(block, plane, LANES)
        slope_two[pl.ds(at, block)] = (1.0 - act_two * act_two).reshape(block, plane, LANES)
        post[pl.ds(at + 1, block)] = after.reshape(block, plane, LANES)
        return carry

    lax.fori_loop(0, rows_x // block, rows, 0, unroll=2)


def primal_stream(post, sides, mirror, write, z_depth):
    rows_x = post.shape[0] - 2
    lane, at_y = lane_iota(ROWS_Y), sublane_iota(ROWS_Y)
    plus_x, minus_x = (lane >= 18) & (lane < 27), lane < 9
    step_y, step_z = lane // 3 % 3, lane % 3
    turn = jnp.where((lane_iota(LANES) + sublane_iota(LANES) == 26), 1.0, 0.0).astype(jnp.bfloat16)
    turn = jnp.concatenate([turn, turn], axis=0)
    for end, z in ((0, 0), (1, z_depth - 1)):
        wall = post[1 : rows_x + 1, z * ROWS_Y : (z + 1) * ROWS_Y, :].reshape(rows_x * ROWS_Y, LANES)
        high, middle = split(wall)
        rest = (wall - high.astype(jnp.float32) - middle.astype(jnp.float32)).astype(jnp.bfloat16)
        turned = dot(jnp.concatenate([high, middle], axis=1), turn) + dot(rest, turn[:LANES])
        mirror[end] = turned.reshape(rows_x, ROWS_Y, LANES)

    def row(x, carry):
        def from_x(take):
            return jnp.where(plus_x, take(x), jnp.where(minus_x, take(x + 2), take(x + 1)))

        low = from_x(lambda i: sides[0, i])
        high = from_x(lambda i: sides[1, i])
        planes = []
        for z in range(z_depth):
            own = from_x(lambda i: post[i, z * ROWS_Y : (z + 1) * ROWS_Y, :])
            up = jnp.where(at_y == 0, low[z : z + 1], pltpu.roll(own, 1, 0))
            down = jnp.where(at_y == ROWS_Y - 1, high[z : z + 1], pltpu.roll(own, ROWS_Y - 1, 0))
            planes.append(jnp.where(step_y == 2, up, jnp.where(step_y == 0, down, own)))
        for z in range(z_depth):
            below = planes[z - 1] if z else mirror[0, x]
            above = planes[z + 1] if z + 1 < z_depth else mirror[1, x]
            write(x, z, jnp.where(step_z == 2, below, jnp.where(step_z == 0, above, planes[z])))
        return carry

    lax.fori_loop(0, rows_x, row, 0, unroll=4)


def jacobians(from_x, to_x, jac, slope_one, slope_two, w_out, mid, pull):
    plane, z_depth = slope_one.shape[1], jac.shape[1]
    lane = lane_iota(CHUNK * plane)
    low_part = (lane >= 2 * QS) & (lane < 3 * QS)

    def row(x, carry):
        one, two = slope_one[x], slope_two[x]

        def finish(first, high, low):
            ready = dot(jnp.concatenate([high, low], axis=1), pull[...])
            ready = jnp.where(low_part, ready - ready.astype(jnp.bfloat16).astype(jnp.float32), ready)
            for i in range(CHUNK):
                for z in range(z_depth):
                    at = i * plane + z * ROWS_Y
                    jac[x, z, (first + i) * ROWS_Y : (first + i + 1) * ROWS_Y, :] = ready[at : at + ROWS_Y]

        waiting = None
        for first in range(0, 27, CHUNK):
            outer = (w_out[first : first + CHUNK, :][:, None, :] * two[None]).reshape(CHUNK * plane, LANES)
            high, low = split(outer)
            both = dot(jnp.concatenate([high, low], axis=1), mid[...])
            if waiting is not None:
                finish(*waiting)
            middle = both[:, :LANES] + both[:, LANES:]
            middle = (middle.reshape(CHUNK, plane, LANES) * one[None]).reshape(CHUNK * plane, LANES)
            waiting = (first, *split(middle))
        finish(*waiting)
        return carry

    lax.fori_loop(from_x, to_x, row, 0, unroll=8)


def move_columns(x, columns, jac, state, post):
    left = lane_iota(QS) < LANES // 2

    def cell_rows(y, z):
        return jac[x, z, pl.ds(y, QS, stride=ROWS_Y), :].astype(jnp.bfloat16)

    for y, pair in columns:
        cell = state[x, pair, pl.ds(y, QS, stride=ROWS_Y), :]
        high, low = split(cell)
        none = jnp.zeros_like(high)
        parts = []
        for keep in (lambda v: jnp.where(left, v, none), lambda v: jnp.where(left, none, v)):
            parts += [keep(high)] * 3 + [keep(low)]
        rows = jnp.concatenate([cell_rows(y, 2 * pair), cell_rows(y, 2 * pair + 1)], axis=1)
        post[x, pair, pl.ds(y, QS, stride=ROWS_Y), :] = cell + dot(rows, jnp.concatenate(parts, axis=0))


def stream_rows(parts_of_x, before, x_rows, sides, write):
    rows_x, pairs = before.shape[0], before.shape[1]
    rows_y = ROWS_Y
    lane = lane_iota(rows_y)
    left = lane < LANES // 2
    at_y = lax.broadcasted_iota(jnp.int32, (rows_y, LANES), 0)
    def one_row(x, edge):
        for q, (ex, ey, ez) in enumerate(LATTICE):
            parts = []
            for pair in range(pairs):
                if edge == -1 and ex == 1:
                    value = x_rows[0, q - 18, pair]
                elif edge == 1 and ex == -1:
                    value = x_rows[1, q, pair]
                else:
                    value = before[x - ex, pair, q * rows_y : (q + 1) * rows_y, :]
                if ey != 0:
                    j = (ex + 1) * 3 + ez + 1
                    side = sides[0 if ey == 1 else 1, j, pair, pl.ds(x - ex + 1, 1), :]
                    if ey == 1:
                        value = jnp.where(at_y == 0, side, pltpu.roll(value, 1, 0))
                    else:
                        value = jnp.where(at_y == rows_y - 1, side, pltpu.roll(value, rows_y - 1, 0))
                parts.append(value)
            if ez != 0:
                turned = [pltpu.roll(part, LANES // 2, 1) for part in parts]
                mirror = 26 - q
                if ez == 1:
                    wall = before[x, 0, mirror * rows_y : (mirror + 1) * rows_y, :]
                    parts = [jnp.where(left, turned[p - 1] if p else wall, turned[p]) for p in range(pairs)]
                else:
                    wall = before[x, pairs - 1, mirror * rows_y : (mirror + 1) * rows_y, :]
                    parts = [jnp.where(left, turned[p], turned[p + 1] if p + 1 < pairs else wall) for p in range(pairs)]
            write(x, q, parts)

    def inner(x, carry):
        one_row(x, 0)
        return carry

    half = rows_x // 2
    if 0 in parts_of_x:
        one_row(0, -1)
    from_x, to_x = 1 if 0 in parts_of_x else half, rows_x - 1 if 1 in parts_of_x else half
    lax.fori_loop(from_x, to_x, inner, 0, unroll=2 - (to_x - from_x) % 2)
    if 1 in parts_of_x:
        one_row(rows_x - 1, 1)


def kernel(z_depth, probe_cells, probe_counts, cells_in, inflow, w_in_t, b_in, w_mid, b_mid, w_out, b_out,
           tangent, sens, primal_out, jac_out, columns_out, *scratch):
    (cells, lift, mix, drop, mid, pull, slope_one, slope_two, turning, inflow_rows, cell_post, cell_sides, mirror,
     cell_edge, cell_face, cell_edge_in, cell_flat, cell_flat_in, cell_corner_in, jac, state, post_even, post_odd, sens_rows, x_rows, sides,
     edge, face, corner, edge_in, face_in, corner_in, observed, jac_rows, jac_in,
     load_sem, sens_sem, send_sem, recv_sem, jac_send_sem, jac_recv_sem) = scratch
    rows_x, pairs, plane = state.shape[0], state.shape[1], cells.shape[1]
    column, columns_x = lax.axis_index("gx"), lax.axis_size("gx")
    line, lines = lax.axis_index("gy"), lax.axis_size("gy")
    me, peers = column * lines + line, columns_x * lines
    first, last = column == 0, column == columns_x - 1
    end, half = rows_x + 1, rows_x // 2
    posts = (post_even, post_odd)

    def at(dx, dy):
        return (lax.rem(column + dx + columns_x, columns_x), lax.rem(line + dy + lines, lines))

    barrier = pltpu.get_barrier_semaphore()

    def greet(i, carry):
        other = lax.rem(me + i, peers)
        pl.semaphore_signal(barrier, inc=1, device_id=(other // lines, lax.rem(other, lines)),
                            device_id_type=pl.DeviceIdType.MESH)
        return carry

    lax.fori_loop(1, peers, greet, 0)

    boxes = state.reshape(rows_x, pairs, QS, ROWS_Y, LANES)

    def load(x, pair):
        return pltpu.make_async_copy(
            tangent.at[:, x, :, pl.ds(pair * LANES, LANES)], boxes.at[x, pair, pl.ds(0, 27)], load_sem.at[x, pair])

    def start_load(x, carry):
        for pair in range(pairs):
            load(x, pair).start()
        return carry

    lax.fori_loop(0, rows_x, start_load, 0)
    sens_copies = []
    for i in range(3):
        from_y = pl.multiple_of(lax.rem(line + i - 1 + lines, lines) * ROWS_Y, ROWS_Y)
        copy = pltpu.make_async_copy(sens.at[:, pl.ds(from_y, ROWS_Y), :], sens_rows.at[i], sens_sem.at[i])
        copy.start()
        sens_copies.append(copy)

    counter = [0]

    def send(source, target, dx, dy):
        i = counter[0]
        counter[0] += 1
        copy = pltpu.make_async_remote_copy(
            src_ref=source, dst_ref=target, send_sem=send_sem.at[i], recv_sem=recv_sem.at[i],
            device_id=at(dx, dy), device_id_type=pl.DeviceIdType.MESH,
        )
        copy.start()
        return copy

    make_weights(w_in_t, w_mid, w_out, lift, mix, drop, mid, pull)
    biases = (b_in[...], b_mid[...], fill(b_out[...], 1, LANES))
    cells[...] = jnp.zeros(cells.shape, jnp.float32)
    cells[:, :, 0:27] = cells_in[...]

    def clear(x, carry):
        for z in range(z_depth):
            jac[x, z, 27 * ROWS_Y :, :] = jnp.zeros(((QS - 27) * ROWS_Y, LANES), jnp.float32)
        for pair in range(pairs):
            state[x, pair, 27 * ROWS_Y :, :] = jnp.zeros(((QS - 27) * ROWS_Y, LANES), jnp.float32)
        return carry

    lax.fori_loop(0, rows_x, clear, 0)

    def pack_cells(step):
        for x in range(rows_x):
            for way, y in ((0, 0), (1, ROWS_Y - 1)):
                for z in range(z_depth):
                    cell_face[step, way, x, z : z + 1, :] = cell_post[x + 1, z * ROWS_Y + y : z * ROWS_Y + y + 1, :]
                cell_face[step, way, x, z_depth:, :] = jnp.zeros((8 - z_depth, LANES), jnp.float32)
        for way in range(2):
            flat = cell_face[step, way].reshape(rows_x * 8, LANES)
            cell_flat[step, way] = jnp.transpose(fill(flat, LANES, LANES))[:QS]
        cell_edge[step, 0] = cell_post[1]
        cell_edge[step, 1] = cell_post[rows_x]

    def send_cells(step):
        return [
            send(cell_edge.at[step, 1], cell_edge_in.at[step, 0], 1, 0),
            send(cell_edge.at[step, 0], cell_edge_in.at[step, 1], -1, 0),
            send(cell_flat.at[step, 1], cell_flat_in.at[step, 0], 0, 1),
            send(cell_flat.at[step, 0], cell_flat_in.at[step, 1], 0, -1),
            send(cell_face.at[step, 1, rows_x - 1], cell_corner_in.at[step, 0], 1, 1),
            send(cell_face.at[step, 1, 0], cell_corner_in.at[step, 1], -1, 1),
            send(cell_face.at[step, 0, rows_x - 1], cell_corner_in.at[step, 2], 1, -1),
            send(cell_face.at[step, 0, 0], cell_corner_in.at[step, 3], -1, -1),
        ]

    def finish_cells(step, copies):
        for copy in copies:
            copy.wait()
        start = pl.multiple_of(line * ROWS_Y, ROWS_Y)
        around = (lax.rem(start + lines * ROWS_Y - 1, lines * ROWS_Y), lax.rem(start + ROWS_Y, lines * ROWS_Y))
        for z in range(z_depth):
            rows = slice(z * ROWS_Y, (z + 1) * ROWS_Y)
            cell_post[0, rows, :] = jnp.where(
                first, inflow_rows[z, pl.ds(start, ROWS_Y), :], cell_edge_in[step, 0, rows, :])
            for way in range(2):
                cell_sides[way, 0, z : z + 1, :] = jnp.where(
                    first, inflow_rows[z, pl.ds(around[way], 1), :], cell_corner_in[step, 2 * way, z : z + 1, :])
        cell_post[end] = jnp.where(last, cell_post[rows_x], cell_edge_in[step, 1])
        for way in range(2):
            flat = jnp.transpose(fill(cell_flat_in[step, way], LANES, LANES))[: rows_x * 8]
            cell_sides[way, 1:end] = flat.reshape(rows_x, 8, LANES)
            cell_sides[way, end] = jnp.where(
                last, flat[(rows_x - 1) * 8 :], cell_corner_in[step, 2 * way + 1])

    def send_columns(step, part, enter=None):
        stride = pairs * QS * ROWS_Y
        post = posts[step % 2]
        flat = post.reshape(rows_x * stride, LANES)
        here = pl.ds(part * half, half)
        for pair in range(pairs):
            for ex in range(3):
                for ez in range(3):
                    for way, q, y in ((1, ex * 9 + 6 + ez, ROWS_Y - 1), (0, ex * 9 + ez, 0)):
                        from_row = part * half * stride + (pair * QS + q) * ROWS_Y + y
                        face[step, way, ex * 3 + ez, pair, part * half : (part + 1) * half, :] = flat[
                            pl.ds(from_row, half, stride=stride), :]
        copies = enter() if enter else []
        copies.append(send(face.at[step, 1, :, :, here], face_in.at[step, 0, :, :, here], 0, 1))
        copies.append(send(face.at[step, 0, :, :, here], face_in.at[step, 1, :, :, here], 0, -1))
        dx = 1 if part else -1
        x = rows_x - 1 if part else 0
        for pair in range(pairs):
            for j in range(9):
                q = (18 if part else 0) + j
                edge[step, part, j, pair] = post[x, pair, q * ROWS_Y : (q + 1) * ROWS_Y, :]
            for i in range(3):
                r, j = i * pairs + pair, (6 if part else 0) + i
                for way in range(2):
                    corner[step, part, way, r : r + 1, :] = face[step, way, j, pair, x : x + 1, :]
        for way in range(2):
            corner[step, part, way, 3 * pairs :, :] = jnp.zeros((corner.shape[3] - 3 * pairs, LANES), jnp.float32)
        copies.append(send(edge.at[step, part], edge_in.at[step, 1 - part], dx, 0))
        for way in range(2):
            target = corner_in.at[step, 2 * (1 - way) + 1 - part]
            copies.append(send(corner.at[step, part, way], target, dx, 1 if way else -1))
        return copies

    def finish_columns(step, copies):
        post = posts[step % 2]
        for copy in copies:
            copy.wait()
        for pair in range(pairs):
            lanes = slice(pair * LANES, (pair + 1) * LANES)
            for j in range(9):
                own = post[rows_x - 1, pair, j * ROWS_Y : (j + 1) * ROWS_Y, :]
                x_rows[0, j, pair] = jnp.where(first, sens_rows[1, j, :, lanes], edge_in[step, 0, j, pair])
                x_rows[1, j, pair] = jnp.where(last, own, edge_in[step, 1, j, pair])
                for way in range(2):
                    sides[way, j, pair, 1:end] = face_in[step, way, j, pair]
            for way, take in ((0, 6), (1, 0)):
                y = ROWS_Y - 1 if way == 0 else 0
                for i in range(3):
                    r, k = i * pairs + pair, take + i
                    sides[way, 6 + i, pair, 0:1] = jnp.where(
                        first, sens_rows[2 * way, k, y : y + 1, lanes], corner_in[step, 2 * way, r : r + 1, :])
                    sides[way, i, pair, end : end + 1] = jnp.where(
                        last, face_in[step, way, i, pair, rows_x - 1 :, :], corner_in[step, 2 * way + 1, r : r + 1, :])

    inner = [(y, pair) for y in range(1, ROWS_Y - 1) for pair in range(pairs)]
    outer = [(y, pair) for y in (0, ROWS_Y - 1) for pair in range(pairs)]

    def mover(columns, post, loads=False):
        def move(x, carry):
            if loads:
                for pair in range(pairs):
                    load(x, pair).wait()
            move_columns(x, columns, jac, state, post)
            return carry

        return move

    def keep_cells(x, z, value):
        cells[x, z * ROWS_Y : (z + 1) * ROWS_Y, :] = value

    def write_cells(x, z, value):
        primal_out[x, z * ROWS_Y : (z + 1) * ROWS_Y, :] = value[:, :27]

    def keep_columns(x, q, parts):
        for pair in range(pairs):
            state[x, pair, q * ROWS_Y : (q + 1) * ROWS_Y, :] = parts[pair]

    primal_collide(cells, cell_post, slope_one, slope_two, biases, lift, mix, drop)
    turning[...] = jnp.zeros(turning.shape, jnp.float32)
    size_y = inflow.shape[2]
    for z in range(z_depth):
        for from_y in range(0, size_y, LANES):
            many = min(LANES, size_y - from_y)
            turning[18:27, 0:many] = inflow[:, z, from_y : from_y + many]
            inflow_rows[z, from_y : from_y + LANES, :] = jnp.transpose(turning[...])
    for copy in sens_copies:
        copy.wait()

    cell_copies = []

    def enter():
        pl.semaphore_wait(barrier, peers - 1)
        cell_copies.extend(send_cells(0))
        return []

    column_copies = []
    for step in range(STEPS):
        earlier, column_copies = column_copies, []
        for part in range(2):
            jacobians(part * half, (part + 1) * half, jac, slope_one, slope_two, w_out, mid, pull)
            if step == 0 and part == 0:
                pack_cells(0)
            if step:
                if part == 0:
                    finish_columns(step - 1, earlier)
                stream_rows((part,), posts[(step - 1) % 2], x_rows, sides, keep_columns)
            move = mover(outer, posts[step % 2], step == 0)
            lax.fori_loop(part * half, (part + 1) * half, move, 0, unroll=4)
            mover(inner, posts[step % 2])((rows_x - 1) * part, 0)
            column_copies += send_columns(step, part, enter if step + part == 0 else None)
        lax.fori_loop(1, rows_x - 1, mover(inner, posts[step % 2]), 0, unroll=2)
        finish_cells(step, cell_copies)
        if step + 1 < STEPS:
            primal_stream(cell_post, cell_sides, mirror, keep_cells, z_depth)
            primal_collide(cells, cell_post, slope_one, slope_two, biases, lift, mix, drop)
            pack_cells(step + 1)
            cell_copies = send_cells(step + 1)
        else:
            primal_stream(cell_post, cell_sides, mirror, write_cells, z_depth)

    sums = {}
    left = lane_iota(ROWS_Y) < LANES // 2

    def write(x, q, parts):
        for pair in range(pairs):
            columns_out[q, x, :, pair * LANES : (pair + 1) * LANES] = parts[pair]
            if q == 0:
                sums[pair] = [None] * 4
            held = sums[pair]
            for m, factor in enumerate((1,) + LATTICE[q]):
                if factor == 0:
                    continue
                if held[m] is None:
                    held[m] = parts[pair] if factor == 1 else -parts[pair]
                else:
                    held[m] = held[m] + parts[pair] if factor == 1 else held[m] - parts[pair]
            if q == 26:
                for m in (0, 2):
                    even = jnp.where(left, held[m], pltpu.roll(held[m + 1], LANES // 2, 1))
                    odd = jnp.where(left, pltpu.roll(held[m], LANES // 2, 1), held[m + 1])
                    for z, value in ((2 * pair, even), (2 * pair + 1, odd)):
                        observed[m // 2, pl.ds(x * plane + z, ROWS_Y, stride=z_depth), :] = value

    finish_columns(STEPS - 1, column_copies)
    stream_rows((0, 1), posts[(STEPS - 1) % 2], x_rows, sides, write)

    slots = probe_cells.shape[0]

    def probe(peer, rows_out, place_out):
        for slot in range(slots):
            cell = jnp.clip(probe_cells[slot, peer], 0, observed.shape[1] - 1)
            live = slot < probe_counts[0, peer]
            for m in range(2):
                value = observed[m, pl.ds(cell, 1), :]
                rows_out[place_out, slot : slot + 1, m * LANES : (m + 1) * LANES] = jnp.where(live, value, 0.0)

    def share(source, target, other):
        return pltpu.make_async_remote_copy(
            src_ref=source, dst_ref=target, send_sem=jac_send_sem, recv_sem=jac_recv_sem,
            device_id=(other // lines, lax.rem(other, lines)), device_id_type=pl.DeviceIdType.MESH,
        )

    def start_share(i, carry):
        other = lax.rem(me + i, peers)
        probe(other, jac_rows, other)
        share(jac_rows.at[other], jac_in.at[me], other).start()
        return carry

    lax.fori_loop(1, peers, start_share, 0, unroll=4)
    probe(me, jac_in, me)
    everyone = pl.ds(0, peers - 1)
    share(jac_rows.at[everyone], jac_in.at[everyone], lax.rem(me + 1, peers)).wait()
    jac_out[...] = jac_in[...]


def hand_out(primal, jac, tangent, primal_out, jac_out, tangent_out, sem):
    copies = []

    def start(source, target):
        copies.append(pltpu.make_async_copy(source, target, sem.at[len(copies)]))
        copies[-1].start()

    for q in range(0, 27, 3):
        start(tangent.at[pl.ds(q, 3)], tangent_out.at[pl.ds(q, 3)])
    start(primal, primal_out)
    start(jac, jac_out)
    for copy in copies:
        copy.wait()


def shape(*dims):
    return jax.ShapeDtypeStruct(dims, jnp.float32)


def on_device(primal_pops, tangent_pops, inflow_pops, inflow_sens, w_in, b_in, w_mid, b_mid, w_out, b_out,
              probe_cells, probe_counts):
    rows_x, rows_y, z_depth = primal_pops.shape[1:]
    width = tangent_pops.shape[3]
    pairs = width // LANES
    plane = z_depth * rows_y
    size_y = inflow_pops.shape[1]
    padded_y = -(-size_y // LANES) * LANES
    peers, slots = probe_cells.shape[1:]
    columns = 4 * width // z_depth
    corner_rows = -(-3 * pairs // 8) * 8

    cells = jnp.transpose(primal_pops, (1, 3, 2, 0)).reshape(rows_x, plane, 27)
    inflow = jnp.transpose(inflow_pops, (0, 2, 1))
    where_probes = jnp.transpose(probe_cells[0], (1, 0))

    def room(*dims, kind=jnp.float32):
        return pltpu.VMEM(dims, kind)

    def weight(n):
        return room(2 * LANES, n, kind=jnp.bfloat16)

    dma = pltpu.SemaphoreType.DMA
    scratch = [
        room(rows_x, plane, LANES),
        weight(2 * LANES), weight(2 * LANES), weight(2 * LANES), weight(2 * LANES), weight(LANES),
        room(rows_x, plane, LANES),
        room(rows_x, plane, LANES),
        room(LANES, LANES),
        room(z_depth, padded_y, LANES),
        room(rows_x + 2, plane, LANES),
        room(2, rows_x + 2, 8, LANES),
        room(2, rows_x, rows_y, LANES),
        room(STEPS, 2, plane, LANES),
        room(STEPS, 2, rows_x, 8, LANES),
        room(STEPS, 2, plane, LANES),
        room(STEPS, 2, QS, LANES),
        room(STEPS, 2, QS, LANES),
        room(STEPS, 4, 8, LANES),
        room(rows_x, z_depth, QS * rows_y, LANES),
        room(rows_x, pairs, QS * rows_y, LANES),
        room(rows_x, pairs, QS * rows_y, LANES),
        room(rows_x, pairs, QS * rows_y, LANES),
        room(3, 9, rows_y, width),
        room(2, 9, pairs, rows_y, LANES),
        room(2, 9, pairs, rows_x + 8, LANES),
        room(STEPS, 2, 9, pairs, rows_y, LANES),
        room(STEPS, 2, 9, pairs, rows_x, LANES),
        room(STEPS, 2, 2, corner_rows, LANES),
        room(STEPS, 2, 9, pairs, rows_y, LANES),
        room(STEPS, 2, 9, pairs, rows_x, LANES),
        room(STEPS, 4, corner_rows, LANES),
        room(2, rows_x * plane, LANES),
        room(peers, slots, columns),
        room(peers, slots, columns),
        dma((rows_x, pairs)),
        dma((3,)),
        dma((18 * STEPS,)),
        dma((18 * STEPS,)),
        dma,
        dma,
    ]
    smem = pl.BlockSpec(memory_space=pltpu.SMEM)
    vmem = pl.BlockSpec(memory_space=pltpu.VMEM)
    left_out = pl.BlockSpec(memory_space=pl.ANY)
    held = pl.pallas_call(
        functools.partial(kernel, z_depth),
        out_shape=(
            room(rows_x, plane, 27), room(peers, slots, columns), room(*tangent_pops.shape)),
        in_specs=[smem, smem] + [vmem] * 8 + [left_out] * 2,
        out_specs=(vmem,) * 3,
        scratch_shapes=scratch,
        compiler_params=pltpu.CompilerParams(vmem_limit_bytes=VMEM_LIMIT, collective_id=1, has_side_effects=True),
        name="slab",
    )(where_probes, probe_counts, cells, inflow, w_in.T, b_in[None], w_mid, b_mid[None], w_out, b_out[None],
      tangent_pops, inflow_sens)
    primal, jac, tangent = pl.pallas_call(
        hand_out,
        out_shape=(shape(rows_x, plane, 27), shape(peers, slots, columns), shape(*tangent_pops.shape)),
        in_specs=[vmem] * 3,
        out_specs=(left_out,) * 3,
        scratch_shapes=[dma((11,))],
        compiler_params=pltpu.CompilerParams(vmem_limit_bytes=1024 * 1024),
        name="hand_out",
    )(*held)
    primal = jnp.transpose(primal.reshape(rows_x, z_depth, rows_y, 27), (3, 0, 2, 1))
    return primal, tangent, jac[None]


def solution(mesh):
    both = P(("gx", "gy"))
    split_xy = P(None, "gx", "gy", None)
    return jax.shard_map(
        on_device,
        mesh=mesh,
        in_specs=(split_xy, split_xy) + (P(),) * 8 + (both, both),
        out_specs=(split_xy, split_xy, both),
        check_vma=False,
    )
```

```python
import functools

import jax
import jax.numpy as jnp
from jax import lax
from jax.experimental import pallas as pl
from jax.experimental.pallas import tpu as pltpu
from jax.sharding import PartitionSpec as P

STEPS = 2
QS = 32
LANES = 128
ROWS_Y = 8
CHUNK = 9
VMEM_LIMIT = 54 * 1024 * 1024
LATTICE = [(q // 9 - 1, q // 3 % 3 - 1, q % 3 - 1) for q in range(27)]


def split(value):
    high = value.astype(jnp.bfloat16)
    low = (value - high.astype(jnp.float32)).astype(jnp.bfloat16)
    return high, low


def dot(a, b):
    return jnp.dot(a, b, preferred_element_type=jnp.float32)


def lane_iota(rows):
    return lax.broadcasted_iota(jnp.int32, (rows, LANES), 1)


def sublane_iota(rows):
    return lax.broadcasted_iota(jnp.int32, (rows, LANES), 0)


def fill(value, rows, columns):
    if value.shape[1] < columns:
        value = jnp.concatenate([value, jnp.zeros((value.shape[0], columns - value.shape[1]), value.dtype)], axis=1)
    if value.shape[0] < rows:
        value = jnp.concatenate([value, jnp.zeros((rows - value.shape[0], columns), value.dtype)], axis=0)
    return value


def three_products(weight):
    high, low = split(weight)
    return jnp.concatenate(
        [jnp.concatenate([high, low], axis=1), jnp.concatenate([high, jnp.zeros_like(low)], axis=1)], axis=0
    )


def times(value, weight):
    high, low = split(value)
    both = dot(jnp.concatenate([high, low], axis=1), weight[...])
    return both[:, :LANES] + both[:, LANES:]


def make_weights(w_in_t, w_mid, w_out, lift, mix, drop, mid, pull):
    turned_in = fill(w_in_t[...], LANES, LANES)
    lift[...] = three_products(turned_in)
    mix[...] = three_products(jnp.transpose(w_mid[...]))
    drop[...] = three_products(jnp.transpose(fill(w_out[...], LANES, LANES)))
    mid[...] = three_products(w_mid[...])
    top = turned_in[:QS]
    high = top.astype(jnp.bfloat16).astype(jnp.float32)
    wide = jnp.transpose(jnp.concatenate([high, top - high, high, high], axis=0))
    lane = lane_iota(LANES)
    only_high = jnp.where((lane >= QS) & (lane < 2 * QS), 0.0, wide)
    pull[...] = jnp.concatenate([wide, only_high], axis=0).astype(jnp.bfloat16)


def primal_collide(cells, post, slope_one, slope_two, biases, lift, mix, drop):
    rows_x, plane = cells.shape[0], cells.shape[1]
    bias_in, bias_mid, bias_out = biases
    block = 4

    def rows(i, carry):
        at = pl.multiple_of(i * block, block)
        cell = cells[pl.ds(at, block)].reshape(block * plane, LANES)
        act_one = jnp.tanh(times(cell, lift) + bias_in)
        act_two = jnp.tanh(times(act_one, mix) + bias_mid)
        after = cell + times(act_two, drop) + bias_out
        slope_one[pl.ds(at, block)] = (1.0 - act_one * act_one).reshape(block, plane, LANES)
        slope_two[pl.ds(at, block)] = (1.0 - act_two * act_two).reshape(block, plane, LANES)
        post[pl.ds(at + 1, block)] = after.reshape(block, plane, LANES)
        return carry

    lax.fori_loop(0, rows_x // block, rows, 0, unroll=2)


def primal_stream(post, sides, mirror, write, z_depth):
    rows_x = post.shape[0] - 2
    lane, at_y = lane_iota(ROWS_Y), sublane_iota(ROWS_Y)
    plus_x, minus_x = (lane >= 18) & (lane < 27), lane < 9
    step_y, step_z = lane // 3 % 3, lane % 3
    turn = jnp.where((lane_iota(LANES) + sublane_iota(LANES) == 26), 1.0, 0.0).astype(jnp.bfloat16)
    turn = jnp.concatenate([turn, turn], axis=0)
    for end, z in ((0, 0), (1, z_depth - 1)):
        wall = post[1 : rows_x + 1, z * ROWS_Y : (z + 1) * ROWS_Y, :].reshape(rows_x * ROWS_Y, LANES)
        high, middle = split(wall)
        rest = (wall - high.astype(jnp.float32) - middle.astype(jnp.float32)).astype(jnp.bfloat16)
        turned = dot(jnp.concatenate([high, middle], axis=1), turn) + dot(rest, turn[:LANES])
        mirror[end] = turned.reshape(rows_x, ROWS_Y, LANES)

    def row(x, carry):
        def from_x(take):
            return jnp.where(plus_x, take(x), jnp.where(minus_x, take(x + 2), take(x + 1)))

        low = from_x(lambda i: sides[0, i])
        high = from_x(lambda i: sides[1, i])
        planes = []
        for z in range(z_depth):
            own = from_x(lambda i: post[i, z * ROWS_Y : (z + 1) * ROWS_Y, :])
            up = jnp.where(at_y == 0, low[z : z + 1], pltpu.roll(own, 1, 0))
            down = jnp.where(at_y == ROWS_Y - 1, high[z : z + 1], pltpu.roll(own, ROWS_Y - 1, 0))
            planes.append(jnp.where(step_y == 2, up, jnp.where(step_y == 0, down, own)))
        for z in range(z_depth):
            below = planes[z - 1] if z else mirror[0, x]
            above = planes[z + 1] if z + 1 < z_depth else mirror[1, x]
            write(x, z, jnp.where(step_z == 2, below, jnp.where(step_z == 0, above, planes[z])))
        return carry

    lax.fori_loop(0, rows_x, row, 0, unroll=4)


def jacobians(from_x, to_x, jac, slope_one, slope_two, w_out, mid, pull):
    plane, z_depth = slope_one.shape[1], jac.shape[1]
    lane = lane_iota(CHUNK * plane)
    low_part = (lane >= 2 * QS) & (lane < 3 * QS)

    def row(x, carry):
        one, two = slope_one[x], slope_two[x]

        def finish(first, high, low):
            ready = dot(jnp.concatenate([high, low], axis=1), pull[...])
            ready = jnp.where(low_part, ready - ready.astype(jnp.bfloat16).astype(jnp.float32), ready)
            for i in range(CHUNK):
                for z in range(z_depth):
                    at = i * plane + z * ROWS_Y
                    jac[x, z, (first + i) * ROWS_Y : (first + i + 1) * ROWS_Y, :] = ready[at : at + ROWS_Y]

        waiting = None
        for first in range(0, 27, CHUNK):
            outer = (w_out[first : first + CHUNK, :][:, None, :] * two[None]).reshape(CHUNK * plane, LANES)
            high, low = split(outer)
            both = dot(jnp.concatenate([high, low], axis=1), mid[...])
            if waiting is not None:
                finish(*waiting)
            middle = both[:, :LANES] + both[:, LANES:]
            middle = (middle.reshape(CHUNK, plane, LANES) * one[None]).reshape(CHUNK * plane, LANES)
            waiting = (first, *split(middle))
        finish(*waiting)
        return carry

    lax.fori_loop(from_x, to_x, row, 0, unroll=8)


def move_columns(x, columns, jac, state, post):
    left = lane_iota(QS) < LANES // 2

    def cell_rows(y, z):
        return jac[x, z, pl.ds(y, QS, stride=ROWS_Y), :].astype(jnp.bfloat16)

    for y, pair in columns:
        cell = state[x, pair, pl.ds(y, QS, stride=ROWS_Y), :]
        high, low = split(cell)
        none = jnp.zeros_like(high)
        parts = []
        for keep in (lambda v: jnp.where(left, v, none), lambda v: jnp.where(left, none, v)):
            parts += [keep(high)] * 3 + [keep(low)]
        rows = jnp.concatenate([cell_rows(y, 2 * pair), cell_rows(y, 2 * pair + 1)], axis=1)
        post[x, pair, pl.ds(y, QS, stride=ROWS_Y), :] = cell + dot(rows, jnp.concatenate(parts, axis=0))


def stream_rows(parts_of_x, before, x_rows, sides, write):
    rows_x, pairs = before.shape[0], before.shape[1]
    rows_y = ROWS_Y
    lane = lane_iota(rows_y)
    left = lane < LANES // 2
    at_y = lax.broadcasted_iota(jnp.int32, (rows_y, LANES), 0)
    def one_row(x, edge):
        for q, (ex, ey, ez) in enumerate(LATTICE):
            parts = []
            for pair in range(pairs):
                if edge == -1 and ex == 1:
                    value = x_rows[0, q - 18, pair]
                elif edge == 1 and ex == -1:
                    value = x_rows[1, q, pair]
                else:
                    value = before[x - ex, pair, q * rows_y : (q + 1) * rows_y, :]
                if ey != 0:
                    j = (ex + 1) * 3 + ez + 1
                    side = sides[0 if ey == 1 else 1, j, pair, pl.ds(x - ex + 1, 1), :]
                    if ey == 1:
                        value = jnp.where(at_y == 0, side, pltpu.roll(value, 1, 0))
                    else:
                        value = jnp.where(at_y == rows_y - 1, side, pltpu.roll(value, rows_y - 1, 0))
                parts.append(value)
            if ez != 0:
                turned = [pltpu.roll(part, LANES // 2, 1) for part in parts]
                mirror = 26 - q
                if ez == 1:
                    wall = before[x, 0, mirror * rows_y : (mirror + 1) * rows_y, :]
                    parts = [jnp.where(left, turned[p - 1] if p else wall, turned[p]) for p in range(pairs)]
                else:
                    wall = before[x, pairs - 1, mirror * rows_y : (mirror + 1) * rows_y, :]
                    parts = [jnp.where(left, turned[p], turned[p + 1] if p + 1 < pairs else wall) for p in range(pairs)]
            write(x, q, parts)

    def inner(x, carry):
        one_row(x, 0)
        return carry

    half = rows_x // 2
    if 0 in parts_of_x:
        one_row(0, -1)
    from_x, to_x = 1 if 0 in parts_of_x else half, rows_x - 1 if 1 in parts_of_x else half
    lax.fori_loop(from_x, to_x, inner, 0, unroll=7 if (to_x - from_x) % 7 == 0 else 1)
    if 1 in parts_of_x:
        one_row(rows_x - 1, 1)


def kernel(z_depth, probe_cells, probe_counts, cells_in, inflow, w_in_t, b_in, w_mid, b_mid, w_out, b_out,
           tangent, sens, primal_out, jac_out, columns_out, *scratch):
    (cells, lift, mix, drop, mid, pull, slope_one, slope_two, turning, inflow_rows, cell_post, cell_sides, mirror,
     cell_edge, cell_face, cell_edge_in, cell_flat, cell_flat_in, cell_corner_in, jac, state, post_even, post_odd, sens_rows, x_rows, sides,
     edge, face, corner, edge_in, face_in, corner_in, observed, jac_rows, jac_in,
     load_sem, sens_sem, send_sem, recv_sem, jac_send_sem, jac_recv_sem) = scratch
    rows_x, pairs, plane = state.shape[0], state.shape[1], cells.shape[1]
    column, columns_x = lax.axis_index("gx"), lax.axis_size("gx")
    line, lines = lax.axis_index("gy"), lax.axis_size("gy")
    me, peers = column * lines + line, columns_x * lines
    first, last = column == 0, column == columns_x - 1
    end, half = rows_x + 1, rows_x // 2
    posts = (post_even, post_odd)

    def at(dx, dy):
        return (lax.rem(column + dx + columns_x, columns_x), lax.rem(line + dy + lines, lines))

    barrier = pltpu.get_barrier_semaphore()

    def greet(i, carry):
        other = lax.rem(me + i, peers)
        pl.semaphore_signal(barrier, inc=1, device_id=(other // lines, lax.rem(other, lines)),
                            device_id_type=pl.DeviceIdType.MESH)
        return carry

    lax.fori_loop(1, peers, greet, 0)

    boxes = state.reshape(rows_x, pairs, QS, ROWS_Y, LANES)

    def load(x, pair):
        return pltpu.make_async_copy(
            tangent.at[:, x, :, pl.ds(pair * LANES, LANES)], boxes.at[x, pair, pl.ds(0, 27)], load_sem.at[x, pair])

    def start_load(x, carry):
        for pair in range(pairs):
            load(x, pair).start()
        return carry

    lax.fori_loop(0, rows_x, start_load, 0)
    sens_copies = []
    for i in range(3):
        from_y = pl.multiple_of(lax.rem(line + i - 1 + lines, lines) * ROWS_Y, ROWS_Y)
        copy = pltpu.make_async_copy(sens.at[:, pl.ds(from_y, ROWS_Y), :], sens_rows.at[i], sens_sem.at[i])
        copy.start()
        sens_copies.append(copy)

    counter = [0]

    def send(source, target, dx, dy):
        i = counter[0]
        counter[0] += 1
        copy = pltpu.make_async_remote_copy(
            src_ref=source, dst_ref=target, send_sem=send_sem.at[i], recv_sem=recv_sem.at[i],
            device_id=at(dx, dy), device_id_type=pl.DeviceIdType.MESH,
        )
        copy.start()
        return copy

    make_weights(w_in_t, w_mid, w_out, lift, mix, drop, mid, pull)
    biases = (b_in[...], b_mid[...], fill(b_out[...], 1, LANES))
    cells[...] = jnp.zeros(cells.shape, jnp.float32)
    cells[:, :, 0:27] = cells_in[...]

    def clear(x, carry):
        for z in range(z_depth):
            jac[x, z, 27 * ROWS_Y :, :] = jnp.zeros(((QS - 27) * ROWS_Y, LANES), jnp.float32)
        for pair in range(pairs):
            state[x, pair, 27 * ROWS_Y :, :] = jnp.zeros(((QS - 27) * ROWS_Y, LANES), jnp.float32)
        return carry

    lax.fori_loop(0, rows_x, clear, 0)

    def pack_cells(step):
        for x in range(rows_x):
            for way, y in ((0, 0), (1, ROWS_Y - 1)):
                for z in range(z_depth):
                    cell_face[step, way, x, z : z + 1, :] = cell_post[x + 1, z * ROWS_Y + y : z * ROWS_Y + y + 1, :]
                cell_face[step, way, x, z_depth:, :] = jnp.zeros((8 - z_depth, LANES), jnp.float32)
        for way in range(2):
            flat = cell_face[step, way].reshape(rows_x * 8, LANES)
            cell_flat[step, way] = jnp.transpose(fill(flat, LANES, LANES))[:QS]
        cell_edge[step, 0] = cell_post[1]
        cell_edge[step, 1] = cell_post[rows_x]

    def send_cells(step):
        return [
            send(cell_edge.at[step, 1], cell_edge_in.at[step, 0], 1, 0),
            send(cell_edge.at[step, 0], cell_edge_in.at[step, 1], -1, 0),
            send(cell_flat.at[step, 1], cell_flat_in.at[step, 0], 0, 1),
            send(cell_flat.at[step, 0], cell_flat_in.at[step, 1], 0, -1),
            send(cell_face.at[step, 1, rows_x - 1], cell_corner_in.at[step, 0], 1, 1),
            send(cell_face.at[step, 1, 0], cell_corner_in.at[step, 1], -1, 1),
            send(cell_face.at[step, 0, rows_x - 1], cell_corner_in.at[step, 2], 1, -1),
            send(cell_face.at[step, 0, 0], cell_corner_in.at[step, 3], -1, -1),
        ]

    def finish_cells(step, copies):
        for copy in copies:
            copy.wait()
        start = pl.multiple_of(line * ROWS_Y, ROWS_Y)
        around = (lax.rem(start + lines * ROWS_Y - 1, lines * ROWS_Y), lax.rem(start + ROWS_Y, lines * ROWS_Y))
        for z in range(z_depth):
            rows = slice(z * ROWS_Y, (z + 1) * ROWS_Y)
            cell_post[0, rows, :] = jnp.where(
                first, inflow_rows[z, pl.ds(start, ROWS_Y), :], cell_edge_in[step, 0, rows, :])
            for way in range(2):
                cell_sides[way, 0, z : z + 1, :] = jnp.where(
                    first, inflow_rows[z, pl.ds(around[way], 1), :], cell_corner_in[step, 2 * way, z : z + 1, :])
        cell_post[end] = jnp.where(last, cell_post[rows_x], cell_edge_in[step, 1])
        for way in range(2):
            flat = jnp.transpose(fill(cell_flat_in[step, way], LANES, LANES))[: rows_x * 8]
            cell_sides[way, 1:end] = flat.reshape(rows_x, 8, LANES)
            cell_sides[way, end] = jnp.where(
                last, flat[(rows_x - 1) * 8 :], cell_corner_in[step, 2 * way + 1])

    def send_columns(step, part, enter=None):
        stride = pairs * QS * ROWS_Y
        post = posts[step % 2]
        flat = post.reshape(rows_x * stride, LANES)
        here = pl.ds(part * half, half)
        for pair in range(pairs):
            for ex in range(3):
                for ez in range(3):
                    for way, q, y in ((1, ex * 9 + 6 + ez, ROWS_Y - 1), (0, ex * 9 + ez, 0)):
                        from_row = part * half * stride + (pair * QS + q) * ROWS_Y + y
                        face[step, way, ex * 3 + ez, pair, part * half : (part + 1) * half, :] = flat[
                            pl.ds(from_row, half, stride=stride), :]
        copies = enter() if enter else []
        copies.append(send(face.at[step, 1, :, :, here], face_in.at[step, 0, :, :, here], 0, 1))
        copies.append(send(face.at[step, 0, :, :, here], face_in.at[step, 1, :, :, here], 0, -1))
        dx = 1 if part else -1
        x = rows_x - 1 if part else 0
        for pair in range(pairs):
            for j in range(9):
                q = (18 if part else 0) + j
                edge[step, part, j, pair] = post[x, pair, q * ROWS_Y : (q + 1) * ROWS_Y, :]
            for i in range(3):
                r, j = i * pairs + pair, (6 if part else 0) + i
                for way in range(2):
                    corner[step, part, way, r : r + 1, :] = face[step, way, j, pair, x : x + 1, :]
        for way in range(2):
            corner[step, part, way, 3 * pairs :, :] = jnp.zeros((corner.shape[3] - 3 * pairs, LANES), jnp.float32)
        copies.append(send(edge.at[step, part], edge_in.at[step, 1 - part], dx, 0))
        for way in range(2):
            target = corner_in.at[step, 2 * (1 - way) + 1 - part]
            copies.append(send(corner.at[step, part, way], target, dx, 1 if way else -1))
        return copies

    def finish_columns(step, copies):
        post = posts[step % 2]
        for copy in copies:
            copy.wait()
        for pair in range(pairs):
            lanes = slice(pair * LANES, (pair + 1) * LANES)
            for j in range(9):
                own = post[rows_x - 1, pair, j * ROWS_Y : (j + 1) * ROWS_Y, :]
                x_rows[0, j, pair] = jnp.where(first, sens_rows[1, j, :, lanes], edge_in[step, 0, j, pair])
                x_rows[1, j, pair] = jnp.where(last, own, edge_in[step, 1, j, pair])
                for way in range(2):
                    sides[way, j, pair, 1:end] = face_in[step, way, j, pair]
            for way, take in ((0, 6), (1, 0)):
                y = ROWS_Y - 1 if way == 0 else 0
                for i in range(3):
                    r, k = i * pairs + pair, take + i
                    sides[way, 6 + i, pair, 0:1] = jnp.where(
                        first, sens_rows[2 * way, k, y : y + 1, lanes], corner_in[step, 2 * way, r : r + 1, :])
                    sides[way, i, pair, end : end + 1] = jnp.where(
                        last, face_in[step, way, i, pair, rows_x - 1 :, :], corner_in[step, 2 * way + 1, r : r + 1, :])

    inner = [(y, pair) for y in range(1, ROWS_Y - 1) for pair in range(pairs)]
    outer = [(y, pair) for y in (0, ROWS_Y - 1) for pair in range(pairs)]

    def mover(columns, post, loads=False):
        def move(x, carry):
            if loads:
                for pair in range(pairs):
                    load(x, pair).wait()
            move_columns(x, columns, jac, state, post)
            return carry

        return move

    def keep_cells(x, z, value):
        cells[x, z * ROWS_Y : (z + 1) * ROWS_Y, :] = value

    def write_cells(x, z, value):
        primal_out[x, z * ROWS_Y : (z + 1) * ROWS_Y, :] = value[:, :27]

    def keep_columns(x, q, parts):
        for pair in range(pairs):
            state[x, pair, q * ROWS_Y : (q + 1) * ROWS_Y, :] = parts[pair]

    primal_collide(cells, cell_post, slope_one, slope_two, biases, lift, mix, drop)
    turning[...] = jnp.zeros(turning.shape, jnp.float32)
    size_y = inflow.shape[2]
    for z in range(z_depth):
        for from_y in range(0, size_y, LANES):
            many = min(LANES, size_y - from_y)
            turning[18:27, 0:many] = inflow[:, z, from_y : from_y + many]
            inflow_rows[z, from_y : from_y + LANES, :] = jnp.transpose(turning[...])
    for copy in sens_copies:
        copy.wait()

    cell_copies = []

    def enter():
        pl.semaphore_wait(barrier, peers - 1)
        cell_copies.extend(send_cells(0))
        return []

    column_copies = []
    for step in range(STEPS):
        earlier, column_copies = column_copies, []
        for part in range(2):
            jacobians(part * half, (part + 1) * half, jac, slope_one, slope_two, w_out, mid, pull)
            if step == 0 and part == 0:
                pack_cells(0)
            if step:
                if part == 0:
                    finish_columns(step - 1, earlier)
                stream_rows((part,), posts[(step - 1) % 2], x_rows, sides, keep_columns)
            move = mover(outer, posts[step % 2], step == 0)
            lax.fori_loop(part * half, (part + 1) * half, move, 0, unroll=4)
            mover(inner, posts[step % 2])((rows_x - 1) * part, 0)
            column_copies += send_columns(step, part, enter if step + part == 0 else None)
        lax.fori_loop(1, rows_x - 1, mover(inner, posts[step % 2]), 0, unroll=2)
        finish_cells(step, cell_copies)
        if step + 1 < STEPS:
            primal_stream(cell_post, cell_sides, mirror, keep_cells, z_depth)
            primal_collide(cells, cell_post, slope_one, slope_two, biases, lift, mix, drop)
            pack_cells(step + 1)
            cell_copies = send_cells(step + 1)
        else:
            primal_stream(cell_post, cell_sides, mirror, write_cells, z_depth)

    sums = {}
    left = lane_iota(ROWS_Y) < LANES // 2

    def write(x, q, parts):
        for pair in range(pairs):
            columns_out[q, x, :, pair * LANES : (pair + 1) * LANES] = parts[pair]
            if q == 0:
                sums[pair] = [None] * 4
            held = sums[pair]
            for m, factor in enumerate((1,) + LATTICE[q]):
                if factor == 0:
                    continue
                if held[m] is None:
                    held[m] = parts[pair] if factor == 1 else -parts[pair]
                else:
                    held[m] = held[m] + parts[pair] if factor == 1 else held[m] - parts[pair]
            if q == 26:
                for m in (0, 2):
                    even = jnp.where(left, held[m], pltpu.roll(held[m + 1], LANES // 2, 1))
                    odd = jnp.where(left, pltpu.roll(held[m], LANES // 2, 1), held[m + 1])
                    for z, value in ((2 * pair, even), (2 * pair + 1, odd)):
                        observed[m // 2, pl.ds(x * plane + z, ROWS_Y, stride=z_depth), :] = value

    finish_columns(STEPS - 1, column_copies)
    stream_rows((0, 1), posts[(STEPS - 1) % 2], x_rows, sides, write)

    slots = probe_cells.shape[0]

    def probe(peer, rows_out, place_out):
        for slot in range(slots):
            cell = jnp.clip(probe_cells[slot, peer], 0, observed.shape[1] - 1)
            live = slot < probe_counts[0, peer]
            for m in range(2):
                value = observed[m, pl.ds(cell, 1), :]
                rows_out[place_out, slot : slot + 1, m * LANES : (m + 1) * LANES] = jnp.where(live, value, 0.0)

    def share(source, target, other):
        return pltpu.make_async_remote_copy(
            src_ref=source, dst_ref=target, send_sem=jac_send_sem, recv_sem=jac_recv_sem,
            device_id=(other // lines, lax.rem(other, lines)), device_id_type=pl.DeviceIdType.MESH,
        )

    def start_share(i, carry):
        other = lax.rem(me + i, peers)
        probe(other, jac_rows, other)
        share(jac_rows.at[other], jac_in.at[me], other).start()
        return carry

    lax.fori_loop(1, peers, start_share, 0, unroll=4)
    probe(me, jac_in, me)
    everyone = pl.ds(0, peers - 1)
    share(jac_rows.at[everyone], jac_in.at[everyone], lax.rem(me + 1, peers)).wait()
    jac_out[...] = jac_in[...]


def hand_out(primal, jac, tangent, primal_out, jac_out, tangent_out, sem):
    copies = []

    def start(source, target):
        copies.append(pltpu.make_async_copy(source, target, sem.at[len(copies)]))
        copies[-1].start()

    for q in range(0, 27, 3):
        start(tangent.at[pl.ds(q, 3)], tangent_out.at[pl.ds(q, 3)])
    start(primal, primal_out)
    start(jac, jac_out)
    for copy in copies:
        copy.wait()


def shape(*dims):
    return jax.ShapeDtypeStruct(dims, jnp.float32)


def on_device(primal_pops, tangent_pops, inflow_pops, inflow_sens, w_in, b_in, w_mid, b_mid, w_out, b_out,
              probe_cells, probe_counts):
    rows_x, rows_y, z_depth = primal_pops.shape[1:]
    width = tangent_pops.shape[3]
    pairs = width // LANES
    plane = z_depth * rows_y
    size_y = inflow_pops.shape[1]
    padded_y = -(-size_y // LANES) * LANES
    peers, slots = probe_cells.shape[1:]
    columns = 4 * width // z_depth
    corner_rows = -(-3 * pairs // 8) * 8

    cells = jnp.transpose(primal_pops, (1, 3, 2, 0)).reshape(rows_x, plane, 27)
    inflow = jnp.transpose(inflow_pops, (0, 2, 1))
    where_probes = jnp.transpose(probe_cells[0], (1, 0))

    def room(*dims, kind=jnp.float32):
        return pltpu.VMEM(dims, kind)

    def weight(n):
        return room(2 * LANES, n, kind=jnp.bfloat16)

    dma = pltpu.SemaphoreType.DMA
    scratch = [
        room(rows_x, plane, LANES),
        weight(2 * LANES), weight(2 * LANES), weight(2 * LANES), weight(2 * LANES), weight(LANES),
        room(rows_x, plane, LANES),
        room(rows_x, plane, LANES),
        room(LANES, LANES),
        room(z_depth, padded_y, LANES),
        room(rows_x + 2, plane, LANES),
        room(2, rows_x + 2, 8, LANES),
        room(2, rows_x, rows_y, LANES),
        room(STEPS, 2, plane, LANES),
        room(STEPS, 2, rows_x, 8, LANES),
        room(STEPS, 2, plane, LANES),
        room(STEPS, 2, QS, LANES),
        room(STEPS, 2, QS, LANES),
        room(STEPS, 4, 8, LANES),
        room(rows_x, z_depth, QS * rows_y, LANES),
        room(rows_x, pairs, QS * rows_y, LANES),
        room(rows_x, pairs, QS * rows_y, LANES),
        room(rows_x, pairs, QS * rows_y, LANES),
        room(3, 9, rows_y, width),
        room(2, 9, pairs, rows_y, LANES),
        room(2, 9, pairs, rows_x + 8, LANES),
        room(STEPS, 2, 9, pairs, rows_y, LANES),
        room(STEPS, 2, 9, pairs, rows_x, LANES),
        room(STEPS, 2, 2, corner_rows, LANES),
        room(STEPS, 2, 9, pairs, rows_y, LANES),
        room(STEPS, 2, 9, pairs, rows_x, LANES),
        room(STEPS, 4, corner_rows, LANES),
        room(2, rows_x * plane, LANES),
        room(peers, slots, columns),
        room(peers, slots, columns),
        dma((rows_x, pairs)),
        dma((3,)),
        dma((18 * STEPS,)),
        dma((18 * STEPS,)),
        dma,
        dma,
    ]
    smem = pl.BlockSpec(memory_space=pltpu.SMEM)
    vmem = pl.BlockSpec(memory_space=pltpu.VMEM)
    left_out = pl.BlockSpec(memory_space=pl.ANY)
    held = pl.pallas_call(
        functools.partial(kernel, z_depth),
        out_shape=(
            room(rows_x, plane, 27), room(peers, slots, columns), room(*tangent_pops.shape)),
        in_specs=[smem, smem] + [vmem] * 8 + [left_out] * 2,
        out_specs=(vmem,) * 3,
        scratch_shapes=scratch,
        compiler_params=pltpu.CompilerParams(vmem_limit_bytes=VMEM_LIMIT, collective_id=1, has_side_effects=True),
        name="slab",
    )(where_probes, probe_counts, cells, inflow, w_in.T, b_in[None], w_mid, b_mid[None], w_out, b_out[None],
      tangent_pops, inflow_sens)
    primal, jac, tangent = pl.pallas_call(
        hand_out,
        out_shape=(shape(rows_x, plane, 27), shape(peers, slots, columns), shape(*tangent_pops.shape)),
        in_specs=[vmem] * 3,
        out_specs=(left_out,) * 3,
        scratch_shapes=[dma((11,))],
        compiler_params=pltpu.CompilerParams(vmem_limit_bytes=1024 * 1024),
        name="hand_out",
    )(*held)
    primal = jnp.transpose(primal.reshape(rows_x, z_depth, rows_y, 27), (3, 0, 2, 1))
    return primal, tangent, jac[None]


def solution(mesh):
    both = P(("gx", "gy"))
    split_xy = P(None, "gx", "gy", None)
    return jax.shard_map(
        on_device,
        mesh=mesh,
        in_specs=(split_xy, split_xy) + (P(),) * 8 + (both, both),
        out_specs=(split_xy, split_xy, both),
        check_vma=False,
    )
```
